512 devices in a mesh: seq: 32 (over z_lo, y), tp: 16 (over x, z_hi, core).
Axes of the slice: x: 4, y: 8, z: 8 (z_hi: 2, z_lo: 4; z = z_hi * 4 + z_lo), core: 2. Of those that a mesh axis runs over, the one named last changes fastest.
Arguments:
- latents: bfloat16 [4096, 3072], P('seq', 'tp'), may hold values from -6 to 6
- lengths: int32 [2], replicated, may hold values from 1 to 3072, 4096 in all
- t_index: int32 [2], replicated, may hold values from 0 to 6
- mod_scale: float32 [3072], replicated, may hold values from -2 to 2
- q_weight: bfloat16 [3072, 2048], P(None, 'tp'), may hold values from -0.109375 to 0.109375
- k_weight: bfloat16 [3072, 2048], P(None, 'tp'), may hold values from -0.109375 to 0.109375
- v_weight: bfloat16 [3072, 2048], P(None, 'tp'), may hold values from -0.109375 to 0.109375
- out_weight: bfloat16 [2048, 3072], P('tp'), may hold values from -0.1875 to 0.1875
- q_gain: float32 [128], replicated, may hold values from 0.6 to 2.4
- k_gain: float32 [128], replicated, may hold values from 0.6 to 2.4
- student_weight: bfloat16 [3072, 3072], P('tp'), may hold values from -0.15625 to 0.15625
Outputs:
- target: bfloat16 [4096, 3072], P('seq', 'tp')
- student_velocity: bfloat16 [4096, 3072], P('seq', 'tp')
- loss: float32 [], replicated
The draws below stay inside these ranges and needn't reach their ends.
Inputs may be any that keep to these rules, and one draw needn't show every extreme that they name: lengths sum to 4096.
All inputs are finite; a program needn't handle non-finite values.
Results may differ from the reference program's by a relative error of at most 0.024.
Values may be sent and summed in bfloat16 or wider, within the bound.
A program may use at most 64 MiB of HBM per device.

```python
import math
import jax
import jax.numpy as jnp
import numpy as np
from jax import lax

D = 3072
HEAD_DIM = 128
TGRID = 8
IMAGES = 2
INNER = 2048
TOKENS = 4096
MOST = 3072
N_TP = 16


def gain_values(key):
    return jax.random.uniform(key, (HEAD_DIM,), jnp.float32, 0.6, 1.8)


def draw_q_gain(key, part):
    return gain_values(jax.random.fold_in(key, 11))


def draw_k_gain(key, part):
    return gain_values(jax.random.fold_in(key, 23))


def strengthened(values, key, source, target, shards_of, factor):
    owner, partner = [(jnp.arange(values.shape[position]) // (values.shape[position] // shards_of)).reshape([-1 if axis == position else 1 for axis in range(values.ndim)]) for position in (source, target)]
    chosen = jax.random.permutation(key, shards_of)[partner]
    strong = (owner == chosen) | (owner == (partner + shards_of // 2) % shards_of)
    return jnp.where(strong, factor * values, values)


def shard_levels(rng, dims, pieces, least, top_value):
    factor_of, own = 1.0, jax.random.fold_in(rng, 6)
    for position, shards_of in pieces:
        steps = jnp.exp(jax.random.uniform(jax.random.fold_in(own, position), (shards_of,), jnp.float32, least / len(pieces), top_value / len(pieces)))
        factor_of = factor_of * jnp.repeat(steps, dims[position] // shards_of).reshape([-1 if axis == position else 1 for axis in range(len(dims))])
    return factor_of


def split_up(amount, total, limit, slope):
    weights = [(1 << 20) // math.isqrt(standing ** slope) + 1 for standing in range(2, amount + 1)]
    rest, counts = total - limit - (amount - 1), [1] * (amount - 1)
    while rest > 0:
        free = [i for i in range(amount - 1) if counts[i] < limit]
        whole, remaining = sum([weights[i] for i in free]), rest
        for i in free:
            addition = min(limit - counts[i], max(1, remaining * weights[i] // whole), rest)
            counts[i] = counts[i] + addition
            rest = rest - addition
    return np.array([limit] + counts)


def uneven_parts(stream_key, count, total, limit, lean):
    if count == 2:
        one = jax.random.randint(stream_key, (), max(1, total - limit), min(limit, total - 1) + 1)
        return jnp.stack([one, total - one])
    tallies = jnp.asarray(split_up(count, total, limit, lean), jnp.int32)
    twos = (count - 1) // 2
    giver, sink = tallies[1:1 + 2 * twos:2], tallies[2:2 + 2 * twos:2]
    slack = jnp.minimum(giver - 1, limit - sink)
    passed = jax.random.randint(jax.random.fold_in(stream_key, 1), (twos,), 0, 1 << 20) % (slack + 1)
    tallies = tallies.at[1:1 + 2 * twos:2].set(giver - passed).at[2:2 + 2 * twos:2].set(sink + passed)
    return tallies[jax.random.permutation(jax.random.fold_in(stream_key, 2), count)]


def bell_draw(own_key, shape, spread, reach, split=(), kind=jnp.bfloat16):
    drawn = jax.random.normal(own_key, shape, jnp.float32) * spread
    if len(split) > 0:
        drawn = shard_levels(own_key, shape, split, -0.22, 0.18) * drawn
    return jnp.clip(drawn, min=-reach, max=reach).astype(kind)


def noise_with(own_key, dims, deviation, reach, split, heavy, held_as=jnp.bfloat16):
    array = deviation * jax.random.normal(own_key, dims, jnp.float32)
    if split:
        array = array * shard_levels(own_key, dims, split, -0.22, 0.18)
    return jnp.clip(strengthened(array, jax.random.fold_in(own_key, 3), *heavy), -reach, reach).astype(held_as)


def setup_inputs(seed: int = 0) -> dict:
    key_list = jax.random.split(jax.random.key(seed), 12)
    return {
        "latents": bell_draw(key_list[0], (TOKENS, D), 1.0, 6.0, ((0, 32), (1, 16))),
        "lengths": uneven_parts(key_list[1], IMAGES, TOKENS, MOST, 2).astype(jnp.int32),
        "t_index": jax.random.randint(key_list[2], (IMAGES,), 0, TGRID - 1).astype(jnp.int32),
        "mod_scale": jnp.clip(jax.random.uniform(key_list[3], (D,), jnp.float32, -2.0, 2.0), -2.0, 2.0),
        "q_weight": bell_draw(key_list[4], (D, INNER), D ** -0.5, 0.109375, ((1, 16),)),
        "k_weight": bell_draw(key_list[5], (D, INNER), D ** -0.5, 0.109375, ((1, 16),)),
        "v_weight": bell_draw(key_list[6], (D, INNER), D ** -0.5, 0.109375, ((1, 16),)),
        "out_weight": noise_with(key_list[7], (INNER, D), INNER ** -0.5, 0.1875, ((0, 16),), (0, 1, 16, 2.0)),
        "q_gain": draw_q_gain(jax.random.fold_in(key_list[11], 71), 0),
        "k_gain": draw_k_gain(jax.random.fold_in(key_list[11], 71), 0),
        "student_weight": noise_with(key_list[10], (D, D), D ** -0.5, 0.15625, ((0, 16),), (0, 1, 16, 2.0)),
    }


epsilon = 1e-06
kinetic_weight = 0.1

def image_index(positions, image_ends):
    return lax.optimization_barrier(jnp.sum((positions[:, None] >= image_ends[None, :]).astype(jnp.int32), axis=1)).astype(jnp.int32)

def head_norm(projected, gain):
    shaped = projected.reshape(projected.shape[0], -1, gain.shape[0])
    normed = shaped * lax.rsqrt(lax.optimization_barrier(jnp.mean(shaped * shaped, axis=-1, keepdims=True)) + epsilon) * gain
    return normed.astype(jnp.bfloat16)

def grouped_sum(left, right, groups):
    inner_width = left.shape[1] // groups

    def add_group(group, total):
        offset = (group * inner_width).astype(jnp.int32)
        columns = lax.dynamic_slice_in_dim(left, offset, inner_width, 1)
        block_rows = lax.dynamic_slice_in_dim(right, offset, inner_width, 0)
        term = jnp.dot(columns, block_rows, preferred_element_type=jnp.float32).astype(jnp.bfloat16)
        term = lax.optimization_barrier(term)
        return total + term.astype(jnp.float32)
    start_total = jnp.zeros((left.shape[0], right.shape[1]), jnp.float32)
    return lax.fori_loop(0, groups, add_group, start_total)

def attention(queries, key_rows, value_rows, image_of):
    score_scale = 1.0 / math.sqrt(queries.shape[2])
    same_image = image_of[:, None] == image_of[None, :]

    def one_head(triple):
        query_head, key_head, value_head = triple
        scores = jnp.dot(query_head, key_head.T, preferred_element_type=jnp.float32) * score_scale
        scores = jnp.where(same_image, scores, -1e+30)
        highest = lax.optimization_barrier(jnp.max(scores, axis=1, keepdims=True))
        weights = jnp.where(same_image, jnp.exp(scores - highest), 0.0)
        totals = lax.optimization_barrier(jnp.sum(weights, axis=1))
        mixed = jnp.dot(weights.astype(jnp.bfloat16), value_head, preferred_element_type=jnp.float32)
        return (mixed / totals[:, None]).astype(jnp.bfloat16)
    heads_out = lax.map(one_head, (queries.transpose(1, 0, 2), key_rows.transpose(1, 0, 2), value_rows.transpose(1, 0, 2)))
    return heads_out.transpose(1, 0, 2).reshape(queries.shape[0], -1)

def teacher(state, times, image_of, mod_scale, q_weight, k_weight, v_weight, out_weight, q_gain, k_gain):
    state32 = state.astype(jnp.float32)
    normed = state32 * lax.rsqrt(lax.optimization_barrier(jnp.mean(state32 * state32, axis=1, keepdims=True)) + epsilon)
    hidden = (normed * (1.0 + times[:, None] * mod_scale[None, :])).astype(jnp.bfloat16)
    queries = head_norm(jnp.dot(hidden, q_weight, preferred_element_type=jnp.float32), q_gain)
    key_rows = head_norm(jnp.dot(hidden, k_weight, preferred_element_type=jnp.float32), k_gain)
    value_rows = jnp.dot(hidden, v_weight, preferred_element_type=jnp.float32).astype(jnp.bfloat16)
    value_rows = value_rows.reshape(queries.shape)
    mixed = attention(queries, key_rows, value_rows, image_of)
    velocity = grouped_sum(mixed, out_weight, N_TP).astype(jnp.bfloat16)
    return (velocity, hidden)

def reference(latents, lengths, t_index, mod_scale, q_weight, k_weight, v_weight, out_weight, q_gain, k_gain, student_weight):
    positions = jnp.arange(TOKENS, dtype=jnp.int32)
    image_ends = jnp.cumsum(lengths).astype(jnp.int32)
    image_of = image_index(positions, image_ends)
    one_hot = (image_of[:, None] == jnp.arange(IMAGES, dtype=jnp.int32)[None, :]).astype(jnp.float32)
    start_times = lax.optimization_barrier(jnp.sum(one_hot * (t_index.astype(jnp.float32) / TGRID)[None, :], axis=1))
    step_size = 1.0 / TGRID
    first_velocity, first_hidden = teacher(latents, start_times, image_of, mod_scale, q_weight, k_weight, v_weight, out_weight, q_gain, k_gain)
    middle = (latents.astype(jnp.float32) + step_size * first_velocity.astype(jnp.float32)).astype(jnp.bfloat16)
    second_velocity, unused_hidden = teacher(middle, start_times + step_size, image_of, mod_scale, q_weight, k_weight, v_weight, out_weight, q_gain, k_gain)
    target = (0.5 * (first_velocity.astype(jnp.float32) + second_velocity.astype(jnp.float32))).astype(jnp.bfloat16)
    student_velocity = grouped_sum(first_hidden, student_weight, N_TP).astype(jnp.bfloat16)
    student32 = student_velocity.astype(jnp.float32)
    residual = student32 - target.astype(jnp.float32)
    per_token = lax.optimization_barrier(jnp.sum(residual * residual, axis=1)) + kinetic_weight * lax.optimization_barrier(jnp.sum(student32 * student32, axis=1))
    image_sum = lax.optimization_barrier(jnp.sum(one_hot * per_token[:, None], axis=0))
    loss = jnp.mean(image_sum / (lengths.astype(jnp.float32) * D))
    return (target, student_velocity, loss)
```

```python
import math

import jax
import jax.numpy as jnp
from jax import lax
from jax.experimental import pallas as pl
from jax.experimental.pallas import tpu as pltpu
from jax.sharding import Mesh
from jax.sharding import PartitionSpec as P

SEQ = ("seq_0", "seq_1")
TP = ("tp_0", "tp_1", "tp_2")
MESH = pl.DeviceIdType.MESH
F32, BF16 = jnp.float32, jnp.bfloat16
NX, NY, NZ = 4, 8, 4
ROWS, HALF = 128, 64
CHUNK, CHUNKS = 384, 8
WIDTH, INNER, HEAD = 3072, 1024, 128
EPS = 1e-6
KINETIC = 0.1
STEP = 0.125
EXP_SCALE = math.log2(math.e) / math.sqrt(HEAD)
MAX_COPIES = 192


def kernel(
    lengths_ref,
    t_index_ref,
    latents_hbm,
    mod_ref,
    wq_hbm,
    wk_hbm,
    wv_hbm,
    wo_hbm,
    q_gain_ref,
    k_gain_ref,
    ws_hbm,
    target_ref,
    student_ref,
    loss_ref,
    lat,
    half_in,
    wqkv,
    wo,
    ws,
    xbuf,
    wcols,
    qbuf,
    kvbuf,
    obuf,
    esend,
    erecv,
    abuf,
    pbuf,
    vbuf,
    v1buf,
    ssend,
    srecv,
    sx_send,
    sx_recv,
    sz_send,
    sz_recv,
    ubuf,
    acc_qkv,
    acc_o,
    lossbuf,
    local_sem,
    send_sem,
    recv_sem,
):
    z = lax.axis_index("seq_0")
    y = lax.axis_index("seq_1")
    x = lax.axis_index("tp_0")
    zh = lax.axis_index("tp_1")
    c = lax.axis_index("tp_2")
    other = 1 - c

    loads = [
        pltpu.make_async_copy(latents_hbm, lat, local_sem.at[0]),
        pltpu.make_async_copy(wq_hbm, wqkv.at[:, 0:HEAD], local_sem.at[1]),
        pltpu.make_async_copy(wk_hbm, wqkv.at[:, HEAD : 2 * HEAD], local_sem.at[2]),
        pltpu.make_async_copy(wv_hbm, wqkv.at[:, 2 * HEAD : 3 * HEAD], local_sem.at[3]),
        pltpu.make_async_copy(wo_hbm, wo, local_sem.at[4]),
        pltpu.make_async_copy(ws_hbm, ws, local_sem.at[5]),
    ]
    for load in loads:
        load.start()

    barrier = pltpu.get_barrier_semaphore()
    peers = [{"seq_1": lax.rem(y + d, NY)} for d in range(1, NY)]
    peers += [{"seq_0": lax.rem(z + d, NZ)} for d in range(1, NZ)]
    peers += [{"seq_0": lax.rem(z + d, NZ), "tp_1": 1 - zh} for d in range(NZ)]
    peers += [{"tp_0": lax.rem(x + d, NX)} for d in range(1, NX)]
    peers += [{"tp_0": lax.rem(x + d, NX), "tp_2": other} for d in range(NX)]
    for peer in peers:
        pl.semaphore_signal(barrier, inc=1, device_id=peer, device_id_type=MESH)
    pl.semaphore_wait(barrier, len(peers))

    count = [0]
    sends = []

    def slot():
        count[0] += 1
        assert count[0] <= MAX_COPIES
        return count[0] - 1

    def send(src, dst, k, **where):
        copy = pltpu.make_async_remote_copy(
            src_ref=src,
            dst_ref=dst,
            send_sem=send_sem.at[k],
            recv_sem=recv_sem.at[k],
            device_id=where,
            device_id_type=MESH,
        )
        copy.start()
        sends.append(copy)

    def arrived(dst, k, **where):
        pltpu.make_async_remote_copy(
            src_ref=dst,
            dst_ref=dst,
            send_sem=send_sem.at[k],
            recv_sem=recv_sem.at[k],
            device_id=where,
            device_id_type=MESH,
        ).wait_recv()

    def x_at(d):
        return lax.rem(x + d + NX, NX)

    def rows_of(which):
        return pl.ds(pl.multiple_of(which * HALF, HALF), HALF)

    def half_columns(value):
        return jnp.where(c == 0, value[:, 0:192], value[:, 192:384])

    first_length = lengths_ref[0]
    first_t = t_index_ref[0].astype(F32) * STEP
    second_t = t_index_ref[1].astype(F32) * STEP
    row_iota = lax.broadcasted_iota(jnp.int32, (ROWS, 1), 0)
    base = (z * NY + y) * ROWS
    in_first = (base + row_iota) < first_length
    start_times = jnp.where(in_first, first_t, second_t)

    loads[0].wait()
    k = slot()
    send(lat.at[rows_of(other), :], half_in, k, tp_2=other)
    arrived(half_in, k, tp_2=other)
    mine = lat[rows_of(c), :].astype(F32)
    theirs = half_in[...].astype(F32)
    left = jnp.where(c == 0, mine, theirs)
    right = jnp.where(c == 0, theirs, mine)
    own_chunk = 2 * x + zh
    xbuf[own_chunk, rows_of(c), :] = jnp.concatenate([left, right], axis=1).astype(BF16)

    def piece(chunk, which):
        return xbuf.at[chunk, rows_of(which), :]

    k_z = slot()
    send(piece(own_chunk, c), piece(own_chunk, c), k_z, tp_1=1 - zh)
    k_x = [[slot() for _ in range(1, NX)] for _ in range(2)]
    k_c = [slot() for _ in range(CHUNKS)]
    for d in range(1, NX):
        send(piece(own_chunk, c), piece(own_chunk, c), k_x[0][d - 1], tp_0=x_at(d))
    send(piece(own_chunk, c), piece(own_chunk, c), k_c[0], tp_2=other)
    arrivals = [own_chunk]
    for d in range(1, NX):
        chunk = 2 * x_at(-d) + zh
        arrived(piece(chunk, c), k_x[0][d - 1], tp_0=x_at(-d))
        send(piece(chunk, c), piece(chunk, c), k_c[d], tp_2=other)
        arrivals.append(chunk)
    far_chunk = 2 * x + 1 - zh
    arrived(piece(far_chunk, c), k_z, tp_1=1 - zh)
    for d in range(1, NX):
        send(piece(far_chunk, c), piece(far_chunk, c), k_x[1][d - 1], tp_0=x_at(d))
    send(piece(far_chunk, c), piece(far_chunk, c), k_c[NX], tp_2=other)
    arrivals.append(far_chunk)

    for load in loads[1:4]:
        load.wait()

    def project_chunk(number, chunk, state, times, squares):
        modulation = mod_ref[pl.ds(chunk, 1), :]
        squares = squares + jnp.sum(state * state, axis=1, keepdims=True)
        hidden = (state * (1.0 + times * modulation)).astype(BF16)
        weights = wqkv[pl.ds(pl.multiple_of(chunk * CHUNK, CHUNK), CHUNK), :]
        term = jnp.dot(hidden, weights, preferred_element_type=F32)
        if number == 0:
            acc_qkv[...] = term
        else:
            acc_qkv[...] += term
        return squares, hidden

    squares = jnp.zeros((ROWS, 1), F32)
    own_hidden = None

    def latents_chunk(number, squares):
        chunk = arrivals[number]
        arrived(piece(chunk, other), k_c[number], tp_2=other)
        return project_chunk(number, chunk, xbuf[chunk].astype(F32), start_times, squares)

    for number in range(NX + 1):
        squares, hidden = latents_chunk(number, squares)
        if number == 0:
            own_hidden = hidden
    for d in range(1, NX):
        chunk = 2 * x_at(-d) + 1 - zh
        arrived(piece(chunk, c), k_x[1][d - 1], tp_0=x_at(-d))
        send(piece(chunk, c), piece(chunk, c), k_c[NX + d], tp_2=other)
        arrivals.append(chunk)
    for number in range(NX + 1, CHUNKS):
        squares, hidden = latents_chunk(number, squares)

    def head_norm(value, gain):
        return (value * lax.rsqrt(jnp.mean(value * value, axis=1, keepdims=True) + EPS) * gain).astype(BF16)

    eye = lax.broadcasted_iota(jnp.int32, (ROWS, ROWS), 0) == lax.broadcasted_iota(
        jnp.int32, (ROWS, ROWS), 1
    )
    lane_iota = lax.broadcasted_iota(jnp.int32, (1, ROWS), 1)

    def attention(e, inverse, while_waiting):
        scaled = acc_qkv[...] * inverse
        qbuf[e, z] = head_norm(scaled[:, 0:HEAD], q_gain_ref[...])
        kvbuf[e, y, 0] = head_norm(scaled[:, HEAD : 2 * HEAD], k_gain_ref[...])
        kvbuf[e, y, 1] = scaled[:, 2 * HEAD : 3 * HEAD].astype(BF16)
        up, down = lax.rem(y + 1, NY), lax.rem(y + NY - 1, NY)
        k_ring = [[[slot(), slot()] for _ in range(4)] for _ in range(2)]
        k_q = [slot() for _ in range(1, NZ)]

        def part(owner, which):
            return kvbuf.at[e, owner, which]

        def pass_on(owner, which, direction, hop):
            target = up if direction == 0 else down
            send(part(owner, which), part(owner, which), k_ring[direction][hop][which], seq_1=target)

        for which in range(2):
            for direction in range(2):
                pass_on(y, which, direction, 0)
        for d in range(1, NZ):
            send(qbuf.at[e, z], qbuf.at[e, z], k_q[d - 1], seq_0=lax.rem(z + d, NZ))
        while_waiting[0]()

        def take(hop):
            owners = (lax.rem(y + NY - hop, NY), lax.rem(y + hop, NY))
            for which in range(2):
                for direction in range(2):
                    if hop == 4 and which != direction:
                        continue
                    source = down if direction == 0 else up
                    arrived(part(owners[direction], which), k_ring[direction][hop - 1][which], seq_1=source)
                    if hop < 3 or (hop == 3 and which == direction):
                        pass_on(owners[direction], which, direction, hop)
            return owners

        queries_from = [lax.rem(z + d, NZ) for d in range(NZ)]

        def block(owner, first):
            keys, values = kvbuf[e, owner, 0], kvbuf[e, owner, 1]
            both = jnp.concatenate([values, jnp.ones_like(values)], axis=1)
            key_first = ((z * NY + owner) * ROWS + lane_iota) < first_length
            for i in range(NZ):
                query_first = ((i * NY + y) * ROWS + row_iota) < first_length
                scores = lax.dot_general(
                    qbuf[e, i], keys, (((1,), (1,)), ((), ())), preferred_element_type=F32
                )
                same = jnp.logical_xor(query_first, jnp.logical_not(key_first))
                weights = jnp.where(same, jnp.exp2(scores * EXP_SCALE), 0.0).astype(BF16)
                term = jnp.dot(weights, both, preferred_element_type=F32)
                if first:
                    acc_o[i] = term
                else:
                    acc_o[i] += term

        around = take(1)
        for d in range(1, NZ):
            source = lax.rem(z + NZ - d, NZ)
            arrived(qbuf.at[e, source], k_q[d - 1], seq_0=source)
        block(y, True)
        for owner in around:
            block(owner, False)
        for hop in (2, 3):
            for owner in take(hop):
                block(owner, False)
        block(take(4)[0], False)

        k_e = [slot() for _ in range(1, NZ)]
        head16 = lax.broadcasted_iota(jnp.int32, (16, ROWS), 0)

        for i in range(NZ):
            product = acc_o[i]
            total = jnp.sum(jnp.where(eye, product[:, HEAD:], 0.0), axis=0, keepdims=True)
            high = total.astype(BF16).astype(F32)
            low = total - high
            esend[e, i, 0:ROWS, :] = product[:, 0:HEAD].astype(BF16)
            esend[e, i, ROWS : ROWS + 16, :] = jnp.where(
                head16 == 0, high, jnp.where(head16 == 1, low, 0.0)
            ).astype(BF16)
        for d in range(1, NZ):
            target = lax.rem(z + d, NZ)
            send(esend.at[e, target], erecv.at[e, d - 1], k_e[d - 1], seq_0=target)
        while_waiting[1]()

        mixed = esend[e, z].astype(F32)
        for d in range(1, NZ):
            arrived(erecv.at[e, d - 1], k_e[d - 1], seq_0=lax.rem(z + NZ - d, NZ))
            mixed = mixed + erecv[e, d - 1].astype(F32)
        total = mixed[ROWS : ROWS + 1, :] + mixed[ROWS + 1 : ROWS + 2, :]
        column = jnp.sum(jnp.where(eye, total, 0.0), axis=1, keepdims=True)
        return (mixed[0:ROWS, :] / column).astype(BF16)

    def velocity(e, attended, while_waiting):
        abuf[e, 2 * x + c] = attended
        k_a = [[slot(), slot()] for _ in range(NX)]
        for d in range(NX):
            for flip in range(2):
                if d == 0 and flip == 0:
                    continue
                send(
                    abuf.at[e, 2 * x + c],
                    abuf.at[e, 2 * x + c],
                    k_a[d][flip],
                    tp_0=x_at(d),
                    tp_2=c if flip == 0 else other,
                )
        while_waiting[0]()
        for d in range(NX):
            for flip in range(2):
                if d == 0 and flip == 0:
                    continue
                core = c if flip == 0 else other
                arrived(abuf.at[e, 2 * x_at(-d) + core], k_a[d][flip], tp_0=x_at(-d), tp_2=core)
        heads = jnp.concatenate([abuf[e, i] for i in range(CHUNKS)], axis=1)
        partial = jnp.dot(heads, wcols[...].reshape(INNER, CHUNK), preferred_element_type=F32)
        pbuf[e, 0] = partial.astype(BF16)
        k_p = slot()
        send(pbuf.at[e, 0], pbuf.at[e, 1], k_p, tp_1=1 - zh)
        while_waiting[1]()
        arrived(pbuf.at[e, 1], k_p, tp_1=1 - zh)
        return (pbuf[e, 0].astype(F32) + pbuf[e, 1].astype(F32)).astype(BF16)

    k_w = [[slot(), slot()] for _ in range(NX)]
    k_sc = slot()
    k_sx = [slot() for _ in range(1, NX)]
    k_sz = slot()
    k_su = slot()
    inverse = lax.rsqrt(squares * (1.0 / WIDTH) + EPS)

    def send_columns():
        loads[4].wait()
        for d in range(NX):
            for flip in range(2):
                if d == 0 and flip == 0:
                    continue
                core = c if flip == 0 else other
                columns = pl.ds(pl.multiple_of((2 * x_at(d) + core) * CHUNK, CHUNK), CHUNK)
                send(wo.at[:, columns], wcols.at[2 * x + c], k_w[d][flip], tp_0=x_at(d), tp_2=core)
        wcols[2 * x + c] = wo[:, pl.ds(pl.multiple_of((2 * x + c) * CHUNK, CHUNK), CHUNK)]
        loads[5].wait()
        rows = half_columns(own_hidden.astype(F32)).astype(BF16)
        for j in range(CHUNKS):
            product = jnp.dot(rows, ws[:, j * CHUNK : (j + 1) * CHUNK], preferred_element_type=F32) * inverse
            ssend[0, j] = product[0:HALF].astype(BF16)
            ssend[1, j] = product[HALF:ROWS].astype(BF16)
        send(ssend.at[other], srecv, k_sc, tp_2=other)

    def student_x():
        arrived(srecv, k_sc, tp_2=other)
        for j in range(CHUNKS):
            sx_send[j] = (ssend[c, j].astype(F32) + srecv[j].astype(F32)).astype(BF16)
        for d in range(1, NX):
            send(sx_send.at[pl.ds(2 * x_at(d), 2)], sx_recv.at[d - 1], k_sx[d - 1], tp_0=x_at(d))

    def student_z():
        total = sx_send[pl.ds(2 * x, 2)].astype(F32)
        for d in range(1, NX):
            arrived(sx_recv.at[d - 1], k_sx[d - 1], tp_0=x_at(-d))
            total = total + sx_recv[d - 1].astype(F32)
        sz_send[...] = total.astype(BF16)
        send(sz_send.at[1 - zh], sz_recv, k_sz, tp_1=1 - zh)

    def columns_here():
        for d in range(NX):
            for flip in range(2):
                if d == 0 and flip == 0:
                    continue
                core = c if flip == 0 else other
                arrived(wcols.at[2 * x_at(-d) + core], k_w[d][flip], tp_0=x_at(-d), tp_2=core)

    def student_core():
        arrived(sz_recv, k_sz, tp_1=1 - zh)
        ubuf[c] = (sz_send[zh].astype(F32) + sz_recv[...].astype(F32)).astype(BF16)
        send(ubuf.at[c], ubuf.at[c], k_su, tp_2=other)

    def nothing():
        pass

    attended = attention(0, inverse, (send_columns, student_x))
    first = velocity(0, attended, (columns_here, student_z))

    own_slot = 2 * x + c
    vbuf[own_slot] = first
    k_vx = [slot() for _ in range(1, NX)]
    k_vc = [slot() for _ in range(NX)]
    for d in range(1, NX):
        send(vbuf.at[own_slot], vbuf.at[own_slot], k_vx[d - 1], tp_0=x_at(d))
    send(vbuf.at[own_slot], vbuf.at[own_slot], k_vc[0], tp_2=other)
    squares = jnp.zeros((ROWS, 1), F32)
    times = start_times + STEP

    def state_chunk(number, chunk, squares):
        state = (xbuf[chunk].astype(F32) + STEP * vbuf[chunk].astype(F32)).astype(BF16)
        return project_chunk(number, chunk, state.astype(F32), times, squares)[0]

    squares = state_chunk(0, own_slot, squares)
    arrived(vbuf.at[2 * x + other], k_vc[0], tp_2=other)
    squares = state_chunk(1, 2 * x + other, squares)
    student_core()
    for d in range(1, NX):
        theirs = 2 * x_at(-d) + c
        arrived(vbuf.at[theirs], k_vx[d - 1], tp_0=x_at(-d))
        send(vbuf.at[theirs], vbuf.at[theirs], k_vc[d], tp_2=other)
        squares = state_chunk(2 * d, theirs, squares)
        if d > 1:
            last = 2 * x_at(1 - d) + other
            arrived(vbuf.at[last], k_vc[d - 1], tp_2=other)
            squares = state_chunk(2 * d - 1, last, squares)
    last = 2 * x_at(1 - NX) + other
    arrived(vbuf.at[last], k_vc[NX - 1], tp_2=other)
    squares = state_chunk(7, last, squares)

    inverse = lax.rsqrt(squares * (1.0 / WIDTH) + EPS)
    attended = attention(1, inverse, (nothing, nothing))
    second = velocity(1, attended, (nothing, nothing))
    v1buf[c] = second
    k_v1 = slot()
    send(v1buf.at[c], v1buf.at[c], k_v1, tp_2=other)

    arrived(ubuf.at[other], k_su, tp_2=other)
    student = half_columns(jnp.concatenate([ubuf[0], ubuf[1]], axis=0).astype(F32))
    student_ref[...] = student.astype(BF16)
    start_velocity = half_columns(vbuf[own_chunk].astype(F32))
    arrived(v1buf.at[other], k_v1, tp_2=other)
    end_velocity = half_columns(v1buf[zh].astype(F32))
    target = (0.5 * (start_velocity + end_velocity)).astype(BF16)
    target_ref[...] = target
    residual = student - target.astype(F32)
    per_token = jnp.sum(residual * residual + KINETIC * (student * student), axis=1, keepdims=True)
    first_sum = jnp.sum(jnp.where(in_first, per_token, 0.0), axis=0, keepdims=True)
    second_sum = jnp.sum(jnp.where(in_first, 0.0, per_token), axis=0, keepdims=True)
    lanes = lax.broadcasted_iota(jnp.int32, (8, ROWS), 1)
    sums = jnp.where(lanes == 0, first_sum, jnp.where(lanes == 1, second_sum, 0.0))

    def exchanged(stage, own, others, sums):
        lossbuf[stage, own] = sums
        numbers = [slot() for _ in others]
        for number, (where, target, source) in zip(numbers, others):
            send(lossbuf.at[stage, own], lossbuf.at[stage, own], number, **where(target))
        for number, (where, target, source) in zip(numbers, others):
            index = source[0]
            arrived(lossbuf.at[stage, index], number, **where(source))
        total = lossbuf[stage, 0]
        for i in range(1, 8):
            total = total + lossbuf[stage, i]
        return total

    def over_x(place):
        return {"tp_0": place[1], "tp_2": place[2]}

    def over_y(place):
        return {"seq_1": place[0]}

    def over_z(place):
        return {"tp_1": place[1], "seq_0": place[2]}

    x_others = []
    for d in range(NX):
        for core in (c, other):
            if d == 0 and core is c:
                continue
            x_others.append(
                (over_x, (None, x_at(d), core), (2 * x_at(-d) + core, x_at(-d), core))
            )
    sums = exchanged(0, 2 * x + c, x_others, sums)
    y_others = [
        (over_y, (lax.rem(y + d, NY),), (lax.rem(y + NY - d, NY),)) for d in range(1, NY)
    ]
    sums = exchanged(1, y, y_others, sums)
    z_others = []
    for d in range(NZ):
        for half in (zh, 1 - zh):
            if d == 0 and half is zh:
                continue
            ahead, behind = lax.rem(z + d, NZ), lax.rem(z + NZ - d, NZ)
            z_others.append((over_z, (None, half, ahead), (half * NZ + behind, half, behind)))
    sums = exchanged(2, zh * NZ + z, z_others, sums)
    scale = jnp.where(
        lanes == 0,
        1.0 / (lengths_ref[0].astype(F32) * WIDTH),
        1.0 / (lengths_ref[1].astype(F32) * WIDTH),
    )
    loss_ref[0, 0] = 0.5 * jnp.sum((sums * scale)[0:1, :])

    for copy in sends:
        copy.wait_send()


def on_device(
    latents,
    lengths,
    t_index,
    mod_scale,
    q_weight,
    k_weight,
    v_weight,
    out_weight,
    q_gain,
    k_gain,
    student_weight,
):
    smem = pl.BlockSpec(memory_space=pltpu.SMEM)
    vmem = pl.BlockSpec(memory_space=pltpu.VMEM)
    anywhere = pl.BlockSpec(memory_space=pl.ANY)
    target, student, loss = pl.pallas_call(
        kernel,
        out_shape=(
            jax.ShapeDtypeStruct((ROWS, 192), BF16),
            jax.ShapeDtypeStruct((ROWS, 192), BF16),
            jax.ShapeDtypeStruct((1, 1), F32),
        ),
        in_specs=[smem, smem, anywhere, vmem, anywhere, anywhere, anywhere, anywhere, vmem, vmem, anywhere],
        out_specs=(vmem, vmem, smem),
        scratch_shapes=[
            pltpu.VMEM((ROWS, 192), BF16),
            pltpu.VMEM((HALF, 192), BF16),
            pltpu.VMEM((WIDTH, CHUNK), BF16),
            pltpu.VMEM((ROWS, WIDTH), BF16),
            pltpu.VMEM((192, WIDTH), BF16),
            pltpu.VMEM((CHUNKS, ROWS, CHUNK), BF16),
            pltpu.VMEM((CHUNKS, ROWS, CHUNK), BF16),
            pltpu.VMEM((2, NZ, ROWS, HEAD), BF16),
            pltpu.VMEM((2, NY, 2, ROWS, HEAD), BF16),
            pltpu.VMEM((8, 128), F32),
            pltpu.VMEM((2, NZ, ROWS + 16, HEAD), BF16),
            pltpu.VMEM((2, NZ - 1, ROWS + 16, HEAD), BF16),
            pltpu.VMEM((2, CHUNKS, ROWS, HEAD), BF16),
            pltpu.VMEM((2, 2, ROWS, CHUNK), BF16),
            pltpu.VMEM((CHUNKS, ROWS, CHUNK), BF16),
            pltpu.VMEM((2, ROWS, CHUNK), BF16),
            pltpu.VMEM((2, CHUNKS, HALF, CHUNK), BF16),
            pltpu.VMEM((CHUNKS, HALF, CHUNK), BF16),
            pltpu.VMEM((CHUNKS, HALF, CHUNK), BF16),
            pltpu.VMEM((NX - 1, 2, HALF, CHUNK), BF16),
            pltpu.VMEM((2, HALF, CHUNK), BF16),
            pltpu.VMEM((HALF, CHUNK), BF16),
            pltpu.VMEM((2, HALF, CHUNK), BF16),
            pltpu.VMEM((ROWS, CHUNK), F32),
            pltpu.VMEM((NZ, ROWS, 2 * HEAD), F32),
            pltpu.VMEM((3, 8, 8, 128), F32),
            pltpu.SemaphoreType.DMA((6,)),
            pltpu.SemaphoreType.DMA((MAX_COPIES,)),
            pltpu.SemaphoreType.DMA((MAX_COPIES,)),
        ],
        compiler_params=pltpu.CompilerParams(
            collective_id=0, has_side_effects=True, vmem_limit_bytes=48 * 1024 * 1024
        ),
    )(
        lengths,
        t_index,
        latents,
        mod_scale.reshape(CHUNKS, CHUNK),
        q_weight,
        k_weight,
        v_weight,
        out_weight,
        q_gain.reshape(1, HEAD),
        k_gain.reshape(1, HEAD),
        student_weight,
    )
    return (target, student, loss.reshape(()))


def solution(mesh):
    torus = Mesh(
        mesh.devices.reshape(4, 8, 4, 2, 2), ("seq_0", "seq_1", "tp_0", "tp_1", "tp_2")
    )
    in_specs = (
        P(SEQ, TP),
        P(),
        P(),
        P(),
        P(None, TP),
        P(None, TP),
        P(None, TP),
        P(TP, None),
        P(),
        P(),
        P(TP, None),
    )
    out_specs = (P(SEQ, TP), P(SEQ, TP), P())
    return jax.shard_map(
        on_device, mesh=torus, in_specs=in_specs, out_specs=out_specs, check_vma=False
    )
```

```python
import math

import jax
import jax.numpy as jnp
from jax import lax
from jax.experimental import pallas as pl
from jax.experimental.pallas import tpu as pltpu
from jax.sharding import Mesh
from jax.sharding import PartitionSpec as P

SEQ = ("seq_0", "seq_1")
TP = ("tp_0", "tp_1", "tp_2")
MESH = pl.DeviceIdType.MESH
F32, BF16 = jnp.float32, jnp.bfloat16
NX, NY, NZ = 4, 8, 4
ROWS, HALF = 128, 64
CHUNK, CHUNKS = 384, 8
WIDTH, INNER, HEAD = 3072, 1024, 128
EPS = 1e-6
KINETIC = 0.1
STEP = 0.125
EXP_SCALE = math.log2(math.e) / math.sqrt(HEAD)
MAX_COPIES = 224
VMEM_LIMIT = 67043328


def kernel(
    lengths_ref,
    t_index_ref,
    latents_hbm,
    mod_ref,
    wq_hbm,
    wk_hbm,
    wv_hbm,
    wo_hbm,
    q_gain_ref,
    k_gain_ref,
    ws_hbm,
    target_ref,
    student_ref,
    loss_ref,
    xt,
    wqkv,
    wo,
    ws,
    xbuf,
    wcols,
    qbuf,
    kvbuf,
    obuf,
    esend,
    erecv,
    abuf,
    pbuf,
    vbuf,
    v1buf,
    ssend,
    srecv,
    sx_send,
    sx_recv,
    sz_send,
    sz_recv,
    ubuf,
    acc_qkv,
    acc_o,
    lossbuf,
    local_sem,
    send_sem,
    recv_sem,
):
    z = lax.axis_index("seq_0")
    y = lax.axis_index("seq_1")
    x = lax.axis_index("tp_0")
    zh = lax.axis_index("tp_1")
    c = lax.axis_index("tp_2")
    other = 1 - c

    loads = [
        pltpu.make_async_copy(latents_hbm, xt.at[2 * x + zh, pl.ds(pl.multiple_of(c * 192, 192), 192), :], local_sem.at[0]),
        pltpu.make_async_copy(wq_hbm, wqkv.at[:, 0:HEAD], local_sem.at[1]),
        pltpu.make_async_copy(wk_hbm, wqkv.at[:, HEAD : 2 * HEAD], local_sem.at[2]),
        pltpu.make_async_copy(wv_hbm, wqkv.at[:, 2 * HEAD : 3 * HEAD], local_sem.at[3]),
        pltpu.make_async_copy(wo_hbm, wo, local_sem.at[4]),
        pltpu.make_async_copy(ws_hbm, ws, local_sem.at[5]),
    ]
    for load in loads:
        load.start()

    barrier = pltpu.get_barrier_semaphore()
    peers = [{"seq_1": lax.rem(y + d, NY)} for d in range(1, NY)]
    peers += [{"seq_0": lax.rem(z + d, NZ)} for d in range(1, NZ)]
    peers += [{"seq_0": lax.rem(z + d, NZ), "tp_1": 1 - zh} for d in range(NZ)]
    peers += [{"tp_0": lax.rem(x + d, NX)} for d in range(1, NX)]
    peers += [{"tp_0": lax.rem(x + d, NX), "tp_2": other} for d in range(NX)]
    for peer in peers:
        pl.semaphore_signal(barrier, inc=1, device_id=peer, device_id_type=MESH)
    loads[0].wait()
    pl.semaphore_wait(barrier, len(peers))

    count = [0]
    sends = []

    def slot():
        count[0] += 1
        assert count[0] <= MAX_COPIES
        return count[0] - 1

    def remote(src, dst, k, **where):
        return pltpu.make_async_remote_copy(
            src_ref=src,
            dst_ref=dst,
            send_sem=send_sem.at[k],
            recv_sem=recv_sem.at[k],
            device_id=where,
            device_id_type=MESH,
        )

    def send(src, dst, k, **where):
        copy = remote(src, dst, k, **where)
        copy.start()
        sends.append(copy)

    def arrived(dst, k, **where):
        remote(dst, dst, k, **where).wait_recv()

    def x_at(d):
        return lax.rem(x + d + NX, NX)

    def rows_of(which):
        return pl.ds(pl.multiple_of(which * HALF, HALF), HALF)

    def half_columns(value):
        return jnp.where(c == 0, value[:, 0:192], value[:, 192:384])

    first_length = lengths_ref[0]
    first_t = t_index_ref[0].astype(F32) * STEP
    second_t = t_index_ref[1].astype(F32) * STEP
    row_iota = lax.broadcasted_iota(jnp.int32, (ROWS, 1), 0)
    base = (z * NY + y) * ROWS
    in_first = (base + row_iota) < first_length
    start_times = jnp.where(in_first, first_t, second_t)

    own_chunk = 2 * x + zh

    def piece(chunk, which):
        return xt.at[chunk, pl.ds(pl.multiple_of(which * 192, 192), 192), :]

    k_z = slot()
    send(piece(own_chunk, c), piece(own_chunk, c), k_z, tp_1=1 - zh)
    k_x = [[slot() for _ in range(1, NX)] for _ in range(2)]
    k_c = [slot() for _ in range(CHUNKS)]
    for d in range(1, NX):
        send(piece(own_chunk, c), piece(own_chunk, c), k_x[0][d - 1], tp_0=x_at(d))
    send(piece(own_chunk, c), piece(own_chunk, c), k_c[0], tp_2=other)
    arrivals = [own_chunk]
    for d in range(1, NX):
        chunk = 2 * x_at(-d) + zh
        arrived(piece(chunk, c), k_x[0][d - 1], tp_0=x_at(-d))
        send(piece(chunk, c), piece(chunk, c), k_c[d], tp_2=other)
        arrivals.append(chunk)
    far_chunk = 2 * x + 1 - zh
    arrived(piece(far_chunk, c), k_z, tp_1=1 - zh)
    for d in range(1, NX):
        send(piece(far_chunk, c), piece(far_chunk, c), k_x[1][d - 1], tp_0=x_at(d))
    send(piece(far_chunk, c), piece(far_chunk, c), k_c[NX], tp_2=other)
    arrivals.append(far_chunk)

    for load in loads[1:4]:
        load.wait()

    def project_chunk(number, chunk, state, times, squares):
        modulation = mod_ref[:, pl.ds(pl.multiple_of(chunk * CHUNK, CHUNK), CHUNK)]
        squares = squares + jnp.sum(state * state, axis=1, keepdims=True)
        hidden = (state * (1.0 + times * modulation)).astype(BF16)
        weights = wqkv[pl.ds(pl.multiple_of(chunk * CHUNK, CHUNK), CHUNK), :]
        term = jnp.dot(hidden, weights, preferred_element_type=F32)
        if number == 0:
            acc_qkv[...] = term
        else:
            acc_qkv[...] += term
        return squares, hidden

    squares = jnp.zeros((ROWS, 1), F32)
    own_hidden = None

    def latents_chunk(number, squares):
        chunk = arrivals[number]
        arrived(piece(chunk, other), k_c[number], tp_2=other)
        state = xt[chunk].T
        xbuf[chunk] = state
        return project_chunk(number, chunk, state.astype(F32), start_times, squares)

    for number in range(NX + 1):
        squares, hidden = latents_chunk(number, squares)
        if number == 0:
            own_hidden = hidden
    for d in range(1, NX):
        chunk = 2 * x_at(-d) + 1 - zh
        arrived(piece(chunk, c), k_x[1][d - 1], tp_0=x_at(-d))
        send(piece(chunk, c), piece(chunk, c), k_c[NX + d], tp_2=other)
        arrivals.append(chunk)
    for number in range(NX + 1, CHUNKS):
        squares, hidden = latents_chunk(number, squares)

    def head_norm(value, gain):
        return (value * lax.rsqrt(jnp.mean(value * value, axis=1, keepdims=True) + EPS) * gain).astype(BF16)

    eye = lax.broadcasted_iota(jnp.int32, (ROWS, ROWS), 0) == lax.broadcasted_iota(
        jnp.int32, (ROWS, ROWS), 1
    )
    lane_iota = lax.broadcasted_iota(jnp.int32, (1, ROWS), 1)

    def attention(e, inverse, while_waiting):
        scaled = acc_qkv[...] * inverse
        qbuf[e, z] = head_norm(scaled[:, 0:HEAD], q_gain_ref[...])
        kvbuf[e, y, 0] = head_norm(scaled[:, HEAD : 2 * HEAD], k_gain_ref[...])
        kvbuf[e, y, 1] = scaled[:, 2 * HEAD : 3 * HEAD].astype(BF16)
        up, down = lax.rem(y + 1, NY), lax.rem(y + NY - 1, NY)
        k_ring = [[[slot(), slot()] for _ in range(4)] for _ in range(2)]
        k_q = [slot() for _ in range(1, NZ)]

        def part(owner, which):
            return kvbuf.at[e, owner, which]

        def pass_on(owner, which, direction, hop):
            target = up if direction == 0 else down
            send(part(owner, which), part(owner, which), k_ring[direction][hop][which], seq_1=target)

        for which in range(2):
            for direction in range(2):
                pass_on(y, which, direction, 0)
        for d in range(1, NZ):
            send(qbuf.at[e, z], qbuf.at[e, z], k_q[d - 1], seq_0=lax.rem(z + d, NZ))
        while_waiting[0]()

        def take(hop):
            owners = (lax.rem(y + NY - hop, NY), lax.rem(y + hop, NY))
            for which in range(2):
                for direction in range(2):
                    if hop == 4 and which != direction:
                        continue
                    source = down if direction == 0 else up
                    arrived(part(owners[direction], which), k_ring[direction][hop - 1][which], seq_1=source)
                    if hop < 3 or (hop == 3 and which == direction):
                        pass_on(owners[direction], which, direction, hop)
            return owners

        queries_from = [lax.rem(z + d, NZ) for d in range(NZ)]

        def block(owner, first):
            keys, values = kvbuf[e, owner, 0], kvbuf[e, owner, 1]
            both = jnp.concatenate([values, jnp.ones_like(values)], axis=1)
            key_first = ((z * NY + owner) * ROWS + lane_iota) < first_length
            for i in range(NZ):
                query_first = ((i * NY + y) * ROWS + row_iota) < first_length
                scores = lax.dot_general(
                    qbuf[e, i], keys, (((1,), (1,)), ((), ())), preferred_element_type=F32
                )
                same = jnp.logical_xor(query_first, jnp.logical_not(key_first))
                weights = jnp.where(same, jnp.exp2(scores * EXP_SCALE), 0.0).astype(BF16)
                term = jnp.dot(weights, both, preferred_element_type=F32)
                if first:
                    acc_o[i] = term
                else:
                    acc_o[i] += term

        around = take(1)
        for d in range(1, NZ):
            source = lax.rem(z + NZ - d, NZ)
            arrived(qbuf.at[e, source], k_q[d - 1], seq_0=source)
        block(y, True)
        for owner in around:
            block(owner, False)
        for hop in (2, 3):
            for owner in take(hop):
                block(owner, False)
        block(take(4)[0], False)

        k_e = [slot() for _ in range(1, NZ)]
        head16 = lax.broadcasted_iota(jnp.int32, (16, ROWS), 0)

        for i in range(NZ):
            product = acc_o[i]
            total = jnp.sum(jnp.where(eye, product[:, HEAD:], 0.0), axis=0, keepdims=True)
            high = total.astype(BF16).astype(F32)
            low = total - high
            esend[e, i, 0:ROWS, :] = product[:, 0:HEAD].astype(BF16)
            esend[e, i, ROWS : ROWS + 16, :] = jnp.where(
                head16 == 0, high, jnp.where(head16 == 1, low, 0.0)
            ).astype(BF16)
        for d in range(1, NZ):
            target = lax.rem(z + d, NZ)
            send(esend.at[e, target], erecv.at[e, d - 1], k_e[d - 1], seq_0=target)
        while_waiting[1]()

        mixed = esend[e, z].astype(F32)
        for d in range(1, NZ):
            arrived(erecv.at[e, d - 1], k_e[d - 1], seq_0=lax.rem(z + NZ - d, NZ))
            mixed = mixed + erecv[e, d - 1].astype(F32)
        total = mixed[ROWS : ROWS + 1, :] + mixed[ROWS + 1 : ROWS + 2, :]
        column = jnp.sum(jnp.where(eye, total, 0.0), axis=1, keepdims=True)
        return (mixed[0:ROWS, :] / column).astype(BF16)

    def partial_velocity(e, attended, while_waiting, hand_on):
        own = 2 * x + c
        k_a = [[[slot(), slot()] for _ in range(NX)] for _ in range(2)]
        for h in range(2):
            abuf[e, h, own] = attended[h * HALF : (h + 1) * HALF]
            for d in range(NX):
                for flip in range(2):
                    if d == 0 and flip == 0:
                        continue
                    send(
                        abuf.at[e, h, own],
                        abuf.at[e, h, own],
                        k_a[h][d][flip],
                        tp_0=x_at(d),
                        tp_2=c if flip == 0 else other,
                    )
        while_waiting()
        for h in range(2):
            for d in range(NX):
                for flip in range(2):
                    if d == 0 and flip == 0:
                        continue
                    core = c if flip == 0 else other
                    arrived(
                        abuf.at[e, h, 2 * x_at(-d) + core], k_a[h][d][flip], tp_0=x_at(-d), tp_2=core
                    )
            heads = jnp.concatenate([abuf[e, h, i] for i in range(CHUNKS)], axis=1)
            partial = jnp.dot(heads, wcols[...].reshape(INNER, CHUNK), preferred_element_type=F32)
            pbuf[e, 0, h] = partial.astype(BF16)
            hand_on(h)

    def both_partials(e, h):
        return (pbuf[e, 0, h].astype(F32) + pbuf[e, 1, h].astype(F32)).astype(BF16)

    k_w = [[slot(), slot()] for _ in range(NX)]
    k_sc = slot()
    k_sx = [slot() for _ in range(1, NX)]
    k_sz = slot()
    k_su = slot()
    inverse = lax.rsqrt(squares * (1.0 / WIDTH) + EPS)

    def send_columns():
        loads[4].wait()
        for d in range(NX):
            for flip in range(2):
                if d == 0 and flip == 0:
                    continue
                core = c if flip == 0 else other
                columns = pl.ds(pl.multiple_of((2 * x_at(d) + core) * CHUNK, CHUNK), CHUNK)
                send(wo.at[:, columns], wcols.at[2 * x + c], k_w[d][flip], tp_0=x_at(d), tp_2=core)
        wcols[2 * x + c] = wo[:, pl.ds(pl.multiple_of((2 * x + c) * CHUNK, CHUNK), CHUNK)]
        loads[5].wait()
        rows = half_columns(own_hidden.astype(F32)).astype(BF16)
        for j in range(CHUNKS):
            product = jnp.dot(rows, ws[:, j * CHUNK : (j + 1) * CHUNK], preferred_element_type=F32) * inverse
            ssend[0, j] = product[0:HALF].astype(BF16)
            ssend[1, j] = product[HALF:ROWS].astype(BF16)
        send(ssend.at[other], srecv, k_sc, tp_2=other)

    def student_x():
        arrived(srecv, k_sc, tp_2=other)
        for j in range(CHUNKS):
            sx_send[j] = (ssend[c, j].astype(F32) + srecv[j].astype(F32)).astype(BF16)
        for d in range(1, NX):
            send(sx_send.at[pl.ds(2 * x_at(d), 2)], sx_recv.at[d - 1], k_sx[d - 1], tp_0=x_at(d))

    def student_z():
        total = sx_send[pl.ds(2 * x, 2)].astype(F32)
        for d in range(1, NX):
            arrived(sx_recv.at[d - 1], k_sx[d - 1], tp_0=x_at(-d))
            total = total + sx_recv[d - 1].astype(F32)
        sz_send[...] = total.astype(BF16)
        send(sz_send.at[1 - zh], sz_recv, k_sz, tp_1=1 - zh)

    def columns_here():
        for d in range(NX):
            for flip in range(2):
                if d == 0 and flip == 0:
                    continue
                core = c if flip == 0 else other
                arrived(wcols.at[2 * x_at(-d) + core], k_w[d][flip], tp_0=x_at(-d), tp_2=core)

    def student_core():
        arrived(sz_recv, k_sz, tp_1=1 - zh)
        ubuf[c] = (sz_send[zh].astype(F32) + sz_recv[...].astype(F32)).astype(BF16)
        send(ubuf.at[c], ubuf.at[c], k_su, tp_2=other)

    def nothing():
        pass

    attended = attention(0, inverse, (send_columns, student_x))
    k_p = [[slot(), slot()] for _ in range(2)]

    def to_partner(h):
        send(pbuf.at[0, 0, h], pbuf.at[0, 1, h], k_p[0][h], tp_1=1 - zh)

    partial_velocity(0, attended, columns_here, to_partner)
    student_z()

    own_slot = 2 * x + c
    k_vx = [[slot() for _ in range(1, NX)] for _ in range(2)]
    k_vc = [[slot() for _ in range(NX)] for _ in range(2)]

    def vpart(chunk, h):
        return vbuf.at[chunk, h * HALF : (h + 1) * HALF, :]

    for h in range(2):
        arrived(pbuf.at[0, 1, h], k_p[0][h], tp_1=1 - zh)
        vbuf[own_slot, h * HALF : (h + 1) * HALF, :] = both_partials(0, h)
        for d in range(1, NX):
            send(vpart(own_slot, h), vpart(own_slot, h), k_vx[h][d - 1], tp_0=x_at(d))
        send(vpart(own_slot, h), vpart(own_slot, h), k_vc[h][0], tp_2=other)
    squares = jnp.zeros((ROWS, 1), F32)
    times = start_times + STEP

    def state_chunk(number, chunk, squares):
        state = (xbuf[chunk].astype(F32) + STEP * vbuf[chunk].astype(F32)).astype(BF16)
        return project_chunk(number, chunk, state.astype(F32), times, squares)[0]

    squares = state_chunk(0, own_slot, squares)
    for h in range(2):
        arrived(vpart(2 * x + other, h), k_vc[h][0], tp_2=other)
    squares = state_chunk(1, 2 * x + other, squares)
    student_core()
    for h in range(2):
        for d in range(1, NX):
            theirs = 2 * x_at(-d) + c
            arrived(vpart(theirs, h), k_vx[h][d - 1], tp_0=x_at(-d))
            send(vpart(theirs, h), vpart(theirs, h), k_vc[h][d], tp_2=other)
    for d in range(1, NX):
        squares = state_chunk(2 * d, 2 * x_at(-d) + c, squares)
    for d in range(1, NX):
        last = 2 * x_at(-d) + other
        for h in range(2):
            arrived(vpart(last, h), k_vc[h][d], tp_2=other)
        squares = state_chunk(2 * d + 1, last, squares)

    inverse = lax.rsqrt(squares * (1.0 / WIDTH) + EPS)
    attended = attention(1, inverse, (nothing, nothing))

    adds, helps = c == zh, c != zh
    k_v1 = [slot(), slot()]

    def partner_copy(h):
        return remote(pbuf.at[1, 0, h], pbuf.at[1, 1, h], k_p[1][h], tp_1=1 - zh)

    def sibling_copy(h):
        part = v1buf.at[h * HALF : (h + 1) * HALF, :]
        return remote(part, part, k_v1[h], tp_2=other)

    def to_partner_if_needed(h):
        @pl.when(helps)
        def _():
            partner_copy(h).start()

    partial_velocity(1, attended, nothing, to_partner_if_needed)

    @pl.when(adds)
    def _():
        for h in range(2):
            partner_copy(h).wait_recv()
            v1buf[h * HALF : (h + 1) * HALF, :] = both_partials(1, h)
            sibling_copy(h).start()

    arrived(ubuf.at[other], k_su, tp_2=other)
    student = half_columns(jnp.concatenate([ubuf[0], ubuf[1]], axis=0).astype(F32))
    student_ref[...] = student.T.astype(BF16)
    start_velocity = half_columns(vbuf[own_chunk].astype(F32))

    @pl.when(helps)
    def _():
        for h in range(2):
            sibling_copy(h).wait_recv()
            partner_copy(h).wait_send()

    @pl.when(adds)
    def _():
        for h in range(2):
            sibling_copy(h).wait_send()

    end_velocity = half_columns(v1buf[...].astype(F32))
    target = (0.5 * (start_velocity + end_velocity)).astype(BF16).astype(F32)
    target_ref[...] = target.T.astype(BF16)
    residual = student - target
    per_token = jnp.sum(residual * residual + KINETIC * (student * student), axis=1, keepdims=True)
    first_sum = jnp.sum(jnp.where(in_first, per_token, 0.0), axis=0, keepdims=True)
    second_sum = jnp.sum(jnp.where(in_first, 0.0, per_token), axis=0, keepdims=True)
    lanes = lane_iota
    sums = jnp.where(lanes == 0, first_sum, jnp.where(lanes == 1, second_sum, 0.0))

    def exchanged(stage, own, others, sums):
        lossbuf[stage, own] = sums
        numbers = [slot() for _ in others]
        for number, (where, target, source) in zip(numbers, others):
            send(lossbuf.at[stage, own], lossbuf.at[stage, own], number, **where(target))
        for number, (where, target, source) in zip(numbers, others):
            index = source[0]
            arrived(lossbuf.at[stage, index], number, **where(source))
        total = lossbuf[stage, 0]
        for i in range(1, 8):
            total = total + lossbuf[stage, i]
        return total

    def over_x(place):
        return {"tp_0": place[1], "tp_2": place[2]}

    def over_y(place):
        return {"seq_1": place[0]}

    def over_z(place):
        return {"tp_1": place[1], "seq_0": place[2]}

    x_others = []
    for d in range(NX):
        for core in (c, other):
            if d == 0 and core is c:
                continue
            x_others.append(
                (over_x, (None, x_at(d), core), (2 * x_at(-d) + core, x_at(-d), core))
            )
    sums = exchanged(0, 2 * x + c, x_others, sums)
    y_others = [
        (over_y, (lax.rem(y + d, NY),), (lax.rem(y + NY - d, NY),)) for d in range(1, NY)
    ]
    sums = exchanged(1, y, y_others, sums)
    z_others = []
    for d in range(NZ):
        for half in (zh, 1 - zh):
            if d == 0 and half is zh:
                continue
            ahead, behind = lax.rem(z + d, NZ), lax.rem(z + NZ - d, NZ)
            z_others.append((over_z, (None, half, ahead), (half * NZ + behind, half, behind)))
    sums = exchanged(2, zh * NZ + z, z_others, sums)
    scale = jnp.where(
        lanes == 0,
        1.0 / (lengths_ref[0].astype(F32) * WIDTH),
        1.0 / (lengths_ref[1].astype(F32) * WIDTH),
    )
    loss_ref[0, 0] = 0.5 * jnp.sum(sums * scale)

    for copy in sends:
        copy.wait_send()


def on_device(
    latents,
    lengths,
    t_index,
    mod_scale,
    q_weight,
    k_weight,
    v_weight,
    out_weight,
    q_gain,
    k_gain,
    student_weight,
):
    smem = pl.BlockSpec(memory_space=pltpu.SMEM)
    vmem = pl.BlockSpec(memory_space=pltpu.VMEM)
    anywhere = pl.BlockSpec(memory_space=pl.ANY)
    target, student, loss = pl.pallas_call(
        kernel,
        out_shape=(
            jax.ShapeDtypeStruct((192, ROWS), BF16),
            jax.ShapeDtypeStruct((192, ROWS), BF16),
            jax.ShapeDtypeStruct((1, 1), F32),
        ),
        in_specs=[smem, smem, anywhere, vmem, anywhere, anywhere, anywhere, anywhere, vmem, vmem, anywhere],
        out_specs=(vmem, vmem, smem),
        scratch_shapes=[
            pltpu.VMEM((CHUNKS, CHUNK, ROWS), BF16),
            pltpu.VMEM((WIDTH, CHUNK), BF16),
            pltpu.VMEM((ROWS, WIDTH), BF16),
            pltpu.VMEM((192, WIDTH), BF16),
            pltpu.VMEM((CHUNKS, ROWS, CHUNK), BF16),
            pltpu.VMEM((CHUNKS, ROWS, CHUNK), BF16),
            pltpu.VMEM((2, NZ, ROWS, HEAD), BF16),
            pltpu.VMEM((2, NY, 2, ROWS, HEAD), BF16),
            pltpu.VMEM((8, 128), F32),
            pltpu.VMEM((2, NZ, ROWS + 16, HEAD), BF16),
            pltpu.VMEM((2, NZ - 1, ROWS + 16, HEAD), BF16),
            pltpu.VMEM((2, 2, CHUNKS, HALF, HEAD), BF16),
            pltpu.VMEM((2, 2, 2, HALF, CHUNK), BF16),
            pltpu.VMEM((CHUNKS, ROWS, CHUNK), BF16),
            pltpu.VMEM((ROWS, CHUNK), BF16),
            pltpu.VMEM((2, CHUNKS, HALF, CHUNK), BF16),
            pltpu.VMEM((CHUNKS, HALF, CHUNK), BF16),
            pltpu.VMEM((CHUNKS, HALF, CHUNK), BF16),
            pltpu.VMEM((NX - 1, 2, HALF, CHUNK), BF16),
            pltpu.VMEM((2, HALF, CHUNK), BF16),
            pltpu.VMEM((HALF, CHUNK), BF16),
            pltpu.VMEM((2, HALF, CHUNK), BF16),
            pltpu.VMEM((ROWS, CHUNK), F32),
            pltpu.VMEM((NZ, ROWS, 2 * HEAD), F32),
            pltpu.VMEM((3, 8, 1, 128), F32),
            pltpu.SemaphoreType.DMA((6,)),
            pltpu.SemaphoreType.DMA((MAX_COPIES,)),
            pltpu.SemaphoreType.DMA((MAX_COPIES,)),
        ],
        compiler_params=pltpu.CompilerParams(
            collective_id=0, has_side_effects=True, vmem_limit_bytes=VMEM_LIMIT
        ),
    )(
        lengths,
        t_index,
        latents.T,
        mod_scale.reshape(1, WIDTH),
        q_weight,
        k_weight,
        v_weight,
        out_weight,
        q_gain.reshape(1, HEAD),
        k_gain.reshape(1, HEAD),
        student_weight,
    )
    return (target.T, student.T, loss.reshape(()))


def solution(mesh):
    torus = Mesh(
        mesh.devices.reshape(4, 8, 4, 2, 2), ("seq_0", "seq_1", "tp_0", "tp_1", "tp_2")
    )
    in_specs = (
        P(SEQ, TP),
        P(),
        P(),
        P(),
        P(None, TP),
        P(None, TP),
        P(None, TP),
        P(TP, None),
        P(),
        P(),
        P(TP, None),
    )
    out_specs = (P(SEQ, TP), P(SEQ, TP), P())
    return jax.shard_map(
        on_device, mesh=torus, in_specs=in_specs, out_specs=out_specs, check_vma=False
    )
```

```python
import math

import jax
import jax.numpy as jnp
from jax import lax
from jax.experimental import pallas as pl
from jax.experimental.pallas import tpu as pltpu
from jax.sharding import Mesh
from jax.sharding import PartitionSpec as P

SEQ = ("seq_0", "seq_1")
TP = ("tp_0", "tp_1", "tp_2")
MESH = pl.DeviceIdType.MESH
F32, BF16 = jnp.float32, jnp.bfloat16
NX, NY, NZ = 4, 8, 4
ROWS, HALF = 128, 64
CHUNK, CHUNKS = 384, 8
WIDTH, INNER, HEAD = 3072, 1024, 128
EPS = 1e-6
KINETIC = 0.1
STEP = 0.125
EXP_SCALE = math.log2(math.e) / math.sqrt(HEAD)
MAX_COPIES = 224
VMEM_LIMIT = 67043328


def kernel(
    lengths_hbm,
    t_index_hbm,
    latents_hbm,
    mod_hbm,
    wq_hbm,
    wk_hbm,
    wv_hbm,
    wo_hbm,
    q_gain_hbm,
    k_gain_hbm,
    ws_hbm,
    both_ref,
    loss_ref,
    xt,
    wqkv,
    wo,
    ws,
    xbuf,
    wcols,
    qbuf,
    kvbuf,
    obuf,
    esend,
    erecv,
    abuf,
    pbuf,
    vbuf,
    v1buf,
    ssend,
    srecv,
    sx_send,
    sx_recv,
    sz_send,
    sz_recv,
    ubuf,
    acc_qkv,
    acc_o,
    lossbuf,
    lengths_ref,
    t_index_ref,
    mod_ref,
    q_gain_ref,
    k_gain_ref,
    local_sem,
    send_sem,
    recv_sem,
):
    z = lax.axis_index("seq_0")
    y = lax.axis_index("seq_1")
    x = lax.axis_index("tp_0")
    zh = lax.axis_index("tp_1")
    c = lax.axis_index("tp_2")
    other = 1 - c

    loads = [
        pltpu.make_async_copy(latents_hbm, xt.at[2 * x + zh, pl.ds(pl.multiple_of(c * 192, 192), 192), :], local_sem.at[0]),
        pltpu.make_async_copy(wq_hbm, wqkv.at[:, 0:HEAD], local_sem.at[1]),
        pltpu.make_async_copy(wk_hbm, wqkv.at[:, HEAD : 2 * HEAD], local_sem.at[2]),
        pltpu.make_async_copy(wv_hbm, wqkv.at[:, 2 * HEAD : 3 * HEAD], local_sem.at[3]),
        pltpu.make_async_copy(wo_hbm, wo, local_sem.at[4]),
        pltpu.make_async_copy(ws_hbm, ws, local_sem.at[5]),
        pltpu.make_async_copy(lengths_hbm, lengths_ref, local_sem.at[6]),
        pltpu.make_async_copy(t_index_hbm, t_index_ref, local_sem.at[7]),
        pltpu.make_async_copy(mod_hbm, mod_ref, local_sem.at[8]),
        pltpu.make_async_copy(q_gain_hbm, q_gain_ref, local_sem.at[9]),
        pltpu.make_async_copy(k_gain_hbm, k_gain_ref, local_sem.at[10]),
    ]
    for load in loads[:1] + loads[6:]:
        load.start()

    barrier = pltpu.get_barrier_semaphore()
    peers = [{"seq_1": lax.rem(y + d, NY)} for d in range(1, NY)]
    peers += [{"seq_0": lax.rem(z + d, NZ)} for d in range(1, NZ)]
    peers += [{"seq_0": lax.rem(z + d, NZ), "tp_1": 1 - zh} for d in range(NZ)]
    peers += [{"tp_0": lax.rem(x + d, NX)} for d in range(1, NX)]
    peers += [{"tp_0": lax.rem(x + d, NX), "tp_2": other} for d in range(NX)]
    for peer in peers:
        pl.semaphore_signal(barrier, inc=1, device_id=peer, device_id_type=MESH)
    for load in loads[:1] + loads[6:]:
        load.wait()
    pl.semaphore_wait(barrier, len(peers))

    count = [0]
    sends = []

    def slot():
        count[0] += 1
        assert count[0] <= MAX_COPIES
        return count[0] - 1

    def remote(src, dst, k, **where):
        return pltpu.make_async_remote_copy(
            src_ref=src,
            dst_ref=dst,
            send_sem=send_sem.at[k],
            recv_sem=recv_sem.at[k],
            device_id=where,
            device_id_type=MESH,
        )

    def send(src, dst, k, **where):
        copy = remote(src, dst, k, **where)
        copy.start()
        sends.append(copy)

    def arrived(dst, k, **where):
        remote(dst, dst, k, **where).wait_recv()

    def x_at(d):
        return lax.rem(x + d + NX, NX)

    def rows_of(which):
        return pl.ds(pl.multiple_of(which * HALF, HALF), HALF)

    def half_columns(value):
        return jnp.where(c == 0, value[:, 0:192], value[:, 192:384])

    first_length = lengths_ref[0]
    first_t = t_index_ref[0].astype(F32) * STEP
    second_t = t_index_ref[1].astype(F32) * STEP
    row_iota = lax.broadcasted_iota(jnp.int32, (ROWS, 1), 0)
    base = (z * NY + y) * ROWS
    in_first = (base + row_iota) < first_length
    start_times = jnp.where(in_first, first_t, second_t)

    own_chunk = 2 * x + zh

    def piece(chunk, which, h=None):
        start, size = (which * 192, 192) if h is None else (which * 192 + h * 96, 96)
        return xt.at[chunk, pl.ds(pl.multiple_of(start, size), size), :]

    k_z = [slot(), slot()]
    k_x = [[[slot(), slot()] for _ in range(1, NX)] for _ in range(2)]
    k_c = [slot() for _ in range(CHUNKS)]
    for h in range(2):
        send(piece(own_chunk, c, h), piece(own_chunk, c, h), k_z[h], tp_1=1 - zh)
    for d in range(1, NX):
        send(piece(own_chunk, c), piece(own_chunk, c), k_x[0][d - 1][0], tp_0=x_at(d))
    send(piece(own_chunk, c), piece(own_chunk, c), k_c[0], tp_2=other)
    for load in loads[1:4]:
        load.start()
    arrivals = [own_chunk]
    far_chunk = 2 * x + 1 - zh
    for h in range(2):
        arrived(piece(far_chunk, c, h), k_z[h], tp_1=1 - zh)
        for d in range(1, NX):
            send(piece(far_chunk, c, h), piece(far_chunk, c, h), k_x[1][d - 1][h], tp_0=x_at(d))
    for d in range(1, NX):
        chunk = 2 * x_at(-d) + zh
        arrived(piece(chunk, c), k_x[0][d - 1][0], tp_0=x_at(-d))
        send(piece(chunk, c), piece(chunk, c), k_c[d], tp_2=other)
        arrivals.append(chunk)
    send(piece(far_chunk, c), piece(far_chunk, c), k_c[NX], tp_2=other)
    arrivals.append(far_chunk)
    for load in loads[4:6]:
        load.start()

    for load in loads[1:4]:
        load.wait()

    def project_chunk(number, chunk, state, times, squares):
        modulation = mod_ref[:, pl.ds(pl.multiple_of(chunk * CHUNK, CHUNK), CHUNK)]
        squares = squares + jnp.sum(state * state, axis=1, keepdims=True)
        hidden = (state * (1.0 + times * modulation)).astype(BF16)
        weights = wqkv[pl.ds(pl.multiple_of(chunk * CHUNK, CHUNK), CHUNK), :]
        term = jnp.dot(hidden, weights, preferred_element_type=F32)
        if number == 0:
            acc_qkv[...] = term
        else:
            acc_qkv[...] += term
        return squares, hidden

    squares = jnp.zeros((ROWS, 1), F32)
    own_hidden = None

    def latents_chunk(number, squares):
        chunk = arrivals[number]
        arrived(piece(chunk, other), k_c[number], tp_2=other)
        state = xt[chunk].T
        xbuf[chunk] = state
        return project_chunk(number, chunk, state.astype(F32), start_times, squares)

    for number in range(NX + 1):
        squares, hidden = latents_chunk(number, squares)
        if number == 0:
            own_hidden = hidden
    for d in range(1, NX):
        chunk = 2 * x_at(-d) + 1 - zh
        for h in range(2):
            arrived(piece(chunk, c, h), k_x[1][d - 1][h], tp_0=x_at(-d))
        send(piece(chunk, c), piece(chunk, c), k_c[NX + d], tp_2=other)
        arrivals.append(chunk)
    for number in range(NX + 1, CHUNKS):
        squares, hidden = latents_chunk(number, squares)

    def head_norm(value, gain):
        return (value * lax.rsqrt(jnp.mean(value * value, axis=1, keepdims=True) + EPS) * gain).astype(BF16)

    eye = lax.broadcasted_iota(jnp.int32, (ROWS, ROWS), 0) == lax.broadcasted_iota(
        jnp.int32, (ROWS, ROWS), 1
    )
    lane_iota = lax.broadcasted_iota(jnp.int32, (1, ROWS), 1)

    def attention(e, inverse, while_waiting):
        scaled = acc_qkv[...] * inverse
        qbuf[e, z] = head_norm(scaled[:, 0:HEAD], q_gain_ref[...])
        kvbuf[e, y, 0] = head_norm(scaled[:, HEAD : 2 * HEAD], k_gain_ref[...])
        kvbuf[e, y, 1] = scaled[:, 2 * HEAD : 3 * HEAD].astype(BF16)
        k_ring = [[[slot(), slot()] for _ in range(4)] for _ in range(2)]
        k_q = [slot() for _ in range(1, NZ)]

        def part(owner, which):
            return kvbuf.at[e, owner, which]

        def at(distance):
            return lax.rem(y + distance + NY, NY)

        def pass_on(owner, which, direction, distance, hops):
            target = at(hops if direction == 0 else -hops)
            send(
                part(owner, which), part(owner, which), k_ring[direction][distance - 1][which], seq_1=target
            )

        for hops in (2, 1):
            for which in range(2):
                for direction in range(2):
                    pass_on(y, which, direction, hops, hops)
        for d in range(1, NZ):
            send(qbuf.at[e, z], qbuf.at[e, z], k_q[d - 1], seq_0=lax.rem(z + d, NZ))
        while_waiting[0]()

        came_by = (1, 2, 1, 2)

        def take(distance):
            owners = (at(-distance), at(distance))
            for which in range(2):
                for direction in range(2):
                    if distance == 4 and which != direction:
                        continue
                    hops = came_by[distance - 1]
                    source = at(-hops if direction == 0 else hops)
                    arrived(part(owners[direction], which), k_ring[direction][distance - 1][which], seq_1=source)
                    if distance == 2:
                        pass_on(owners[direction], which, direction, 3, 1)
                        if which == direction:
                            pass_on(owners[direction], which, direction, 4, 2)
            return owners

        queries_from = [lax.rem(z + d, NZ) for d in range(NZ)]

        def block(owner, first):
            keys, values = kvbuf[e, owner, 0], kvbuf[e, owner, 1]
            both = jnp.concatenate([values, jnp.ones_like(values)], axis=1)
            key_first = ((z * NY + owner) * ROWS + lane_iota) < first_length
            for i in range(NZ):
                query_first = ((i * NY + y) * ROWS + row_iota) < first_length
                scores = lax.dot_general(
                    qbuf[e, i], keys, (((1,), (1,)), ((), ())), preferred_element_type=F32
                )
                same = jnp.logical_xor(query_first, jnp.logical_not(key_first))
                weights = jnp.where(same, jnp.exp2(scores * EXP_SCALE), 0.0).astype(BF16)
                term = jnp.dot(weights, both, preferred_element_type=F32)
                if first:
                    acc_o[i] = term
                else:
                    acc_o[i] += term

        near = take(2) + take(1)
        for d in range(1, NZ):
            source = lax.rem(z + NZ - d, NZ)
            arrived(qbuf.at[e, source], k_q[d - 1], seq_0=source)
        block(y, True)
        for owner in near:
            block(owner, False)
        for owner in take(3):
            block(owner, False)
        block(take(4)[0], False)

        k_e = [slot() for _ in range(1, NZ)]
        head16 = lax.broadcasted_iota(jnp.int32, (16, ROWS), 0)

        for i in range(NZ):
            product = acc_o[i]
            total = jnp.sum(jnp.where(eye, product[:, HEAD:], 0.0), axis=0, keepdims=True)
            high = total.astype(BF16).astype(F32)
            low = total - high
            esend[e, i, 0:ROWS, :] = product[:, 0:HEAD].astype(BF16)
            esend[e, i, ROWS : ROWS + 16, :] = jnp.where(
                head16 == 0, high, jnp.where(head16 == 1, low, 0.0)
            ).astype(BF16)
        for d in range(1, NZ):
            target = lax.rem(z + d, NZ)
            send(esend.at[e, target], erecv.at[e, d - 1], k_e[d - 1], seq_0=target)
        while_waiting[1]()

        mixed = esend[e, z].astype(F32)
        for d in range(1, NZ):
            arrived(erecv.at[e, d - 1], k_e[d - 1], seq_0=lax.rem(z + NZ - d, NZ))
            mixed = mixed + erecv[e, d - 1].astype(F32)
        total = mixed[ROWS : ROWS + 1, :] + mixed[ROWS + 1 : ROWS + 2, :]
        column = jnp.sum(jnp.where(eye, total, 0.0), axis=1, keepdims=True)
        return (mixed[0:ROWS, :] / column).astype(BF16)

    def partial_velocity(e, attended, while_waiting, hand_on):
        own = 2 * x + c
        k_a = [[[slot(), slot()] for _ in range(NX)] for _ in range(2)]
        for h in range(2):
            abuf[e, h, own] = attended[h * HALF : (h + 1) * HALF]
            for d in range(NX):
                for flip in range(2):
                    if d == 0 and flip == 0:
                        continue
                    send(
                        abuf.at[e, h, own],
                        abuf.at[e, h, own],
                        k_a[h][d][flip],
                        tp_0=x_at(d),
                        tp_2=c if flip == 0 else other,
                    )
        while_waiting()
        for h in range(2):
            for d in range(NX):
                for flip in range(2):
                    if d == 0 and flip == 0:
                        continue
                    core = c if flip == 0 else other
                    arrived(
                        abuf.at[e, h, 2 * x_at(-d) + core], k_a[h][d][flip], tp_0=x_at(-d), tp_2=core
                    )
            heads = jnp.concatenate([abuf[e, h, i] for i in range(CHUNKS)], axis=1)
            partial = jnp.dot(heads, wcols[...].reshape(INNER, CHUNK), preferred_element_type=F32)
            pbuf[e, 0, h] = partial.astype(BF16)
            hand_on(h)

    def both_partials(e, h):
        return (pbuf[e, 0, h].astype(F32) + pbuf[e, 1, h].astype(F32)).astype(BF16)

    k_w = [[slot(), slot()] for _ in range(NX)]
    k_sc = slot()
    k_sx = [slot() for _ in range(1, NX)]
    k_sz = slot()
    k_su = slot()
    inverse = lax.rsqrt(squares * (1.0 / WIDTH) + EPS)

    def send_columns():
        loads[4].wait()
        for d in range(NX):
            for flip in range(2):
                if d == 0 and flip == 0:
                    continue
                core = c if flip == 0 else other
                columns = pl.ds(pl.multiple_of((2 * x_at(d) + core) * CHUNK, CHUNK), CHUNK)
                send(wo.at[:, columns], wcols.at[2 * x + c], k_w[d][flip], tp_0=x_at(d), tp_2=core)
        wcols[2 * x + c] = wo[:, pl.ds(pl.multiple_of((2 * x + c) * CHUNK, CHUNK), CHUNK)]
        loads[5].wait()
        rows = half_columns(own_hidden.astype(F32)).astype(BF16)
        for j in range(CHUNKS):
            product = jnp.dot(rows, ws[:, j * CHUNK : (j + 1) * CHUNK], preferred_element_type=F32) * inverse
            ssend[0, j] = product[0:HALF].astype(BF16)
            ssend[1, j] = product[HALF:ROWS].astype(BF16)
        send(ssend.at[other], srecv, k_sc, tp_2=other)

    def student_x():
        arrived(srecv, k_sc, tp_2=other)
        for j in range(CHUNKS):
            sx_send[j] = (ssend[c, j].astype(F32) + srecv[j].astype(F32)).astype(BF16)
        for d in range(1, NX):
            send(sx_send.at[pl.ds(2 * x_at(d), 2)], sx_recv.at[d - 1], k_sx[d - 1], tp_0=x_at(d))

    def student_z():
        total = sx_send[pl.ds(2 * x, 2)].astype(F32)
        for d in range(1, NX):
            arrived(sx_recv.at[d - 1], k_sx[d - 1], tp_0=x_at(-d))
            total = total + sx_recv[d - 1].astype(F32)
        sz_send[...] = total.astype(BF16)
        send(sz_send.at[1 - zh], sz_recv, k_sz, tp_1=1 - zh)

    def columns_here():
        for d in range(NX):
            for flip in range(2):
                if d == 0 and flip == 0:
                    continue
                core = c if flip == 0 else other
                arrived(wcols.at[2 * x_at(-d) + core], k_w[d][flip], tp_0=x_at(-d), tp_2=core)

    def student_core():
        arrived(sz_recv, k_sz, tp_1=1 - zh)
        ubuf[c] = (sz_send[zh].astype(F32) + sz_recv[...].astype(F32)).astype(BF16)
        send(ubuf.at[c], ubuf.at[c], k_su, tp_2=other)

    def nothing():
        pass

    attended = attention(0, inverse, (send_columns, student_x))
    k_p = [[slot(), slot()] for _ in range(2)]

    def to_partner(h):
        send(pbuf.at[0, 0, h], pbuf.at[0, 1, h], k_p[0][h], tp_1=1 - zh)

    partial_velocity(0, attended, columns_here, to_partner)
    student_z()

    own_slot = 2 * x + c
    k_vx = [[slot() for _ in range(1, NX)] for _ in range(2)]
    k_vc = [[slot() for _ in range(NX)] for _ in range(2)]

    def vpart(chunk, h):
        return vbuf.at[chunk, h * HALF : (h + 1) * HALF, :]

    for h in range(2):
        arrived(pbuf.at[0, 1, h], k_p[0][h], tp_1=1 - zh)
        vbuf[own_slot, h * HALF : (h + 1) * HALF, :] = both_partials(0, h)
        for d in range(1, NX):
            send(vpart(own_slot, h), vpart(own_slot, h), k_vx[h][d - 1], tp_0=x_at(d))
        send(vpart(own_slot, h), vpart(own_slot, h), k_vc[h][0], tp_2=other)
    squares = jnp.zeros((ROWS, 1), F32)
    times = start_times + STEP

    def state_chunk(number, chunk, squares):
        state = (xbuf[chunk].astype(F32) + STEP * vbuf[chunk].astype(F32)).astype(BF16)
        return project_chunk(number, chunk, state.astype(F32), times, squares)[0]

    squares = state_chunk(0, own_slot, squares)
    for h in range(2):
        arrived(vpart(2 * x + other, h), k_vc[h][0], tp_2=other)
    squares = state_chunk(1, 2 * x + other, squares)
    for h in range(2):
        for d in range(1, NX):
            theirs = 2 * x_at(-d) + c
            arrived(vpart(theirs, h), k_vx[h][d - 1], tp_0=x_at(-d))
            send(vpart(theirs, h), vpart(theirs, h), k_vc[h][d], tp_2=other)
    for d in range(1, NX):
        squares = state_chunk(2 * d, 2 * x_at(-d) + c, squares)
    for d in range(1, NX):
        last = 2 * x_at(-d) + other
        for h in range(2):
            arrived(vpart(last, h), k_vc[h][d], tp_2=other)
        squares = state_chunk(2 * d + 1, last, squares)

    inverse = lax.rsqrt(squares * (1.0 / WIDTH) + EPS)
    attended = attention(1, inverse, (student_core, nothing))

    adds, helps = c == zh, c != zh
    k_v1 = [slot(), slot()]

    def partner_copy(h):
        return remote(pbuf.at[1, 0, h], pbuf.at[1, 1, h], k_p[1][h], tp_1=1 - zh)

    def sibling_copy(h):
        part = v1buf.at[h * HALF : (h + 1) * HALF, :]
        return remote(part, part, k_v1[h], tp_2=other)

    def to_partner_if_needed(h):
        @pl.when(helps)
        def _():
            partner_copy(h).start()

    partial_velocity(1, attended, nothing, to_partner_if_needed)

    arrived(ubuf.at[other], k_su, tp_2=other)
    student_whole = jnp.concatenate([ubuf[0], ubuf[1]], axis=0).astype(F32)
    start_whole = vbuf[own_chunk].astype(F32)
    lanes = lane_iota
    k_l = [[slot(), slot()] for _ in range(NX)]

    def loss_row(d, flip):
        row = lossbuf.at[0, x]
        return remote(row, row, k_l[d][flip], tp_0=x_at(d), tp_2=c if flip == 0 else other)

    def loss_row_from(d, flip):
        row = lossbuf.at[0, x_at(-d)]
        return remote(row, row, k_l[d][flip], tp_0=x_at(-d), tp_2=c if flip == 0 else other)

    @pl.when(adds)
    def _():
        for h in range(2):
            partner_copy(h).wait_recv()
            v1buf[h * HALF : (h + 1) * HALF, :] = both_partials(1, h)
            sibling_copy(h).start()
        whole = (0.5 * (start_whole + v1buf[...].astype(F32))).astype(BF16).astype(F32)
        residual = student_whole - whole
        per_token = jnp.sum(
            residual * residual + KINETIC * (student_whole * student_whole), axis=1, keepdims=True
        )
        first_sum = jnp.sum(jnp.where(in_first, per_token, 0.0), axis=0, keepdims=True)
        second_sum = jnp.sum(jnp.where(in_first, 0.0, per_token), axis=0, keepdims=True)
        lossbuf[0, x] = jnp.where(lanes == 0, first_sum, jnp.where(lanes == 1, second_sum, 0.0))
        for d in range(NX):
            for flip in range(2):
                if d or flip:
                    loss_row(d, flip).start()

    both_ref[1] = half_columns(student_whole).T.astype(BF16)

    @pl.when(helps)
    def _():
        for h in range(2):
            sibling_copy(h).wait_recv()
            partner_copy(h).wait_send()
        for d in range(NX):
            loss_row_from(d, 1).wait_recv()

    @pl.when(adds)
    def _():
        for d in range(1, NX):
            loss_row_from(d, 0).wait_recv()

    sums = lossbuf[0, 0]
    for i in range(1, NX):
        sums = sums + lossbuf[0, i]

    def exchanged(stage, own, others, sums):
        lossbuf[stage, own] = sums
        numbers = [slot() for _ in others]
        for number, (where, target, source) in zip(numbers, others):
            send(lossbuf.at[stage, own], lossbuf.at[stage, own], number, **where(target))
        if stage == 1:
            both_ref[0] = half_columns(0.5 * (start_whole + v1buf[...].astype(F32))).T.astype(BF16)
        for number, (where, target, source) in zip(numbers, others):
            index = source[0]
            arrived(lossbuf.at[stage, index], number, **where(source))
        total = lossbuf[stage, 0]
        for i in range(1, 8):
            total = total + lossbuf[stage, i]
        return total

    def over_y(place):
        return {"seq_1": place[0]}

    def over_z(place):
        return {"tp_1": place[1], "seq_0": place[2]}

    y_others = [
        (over_y, (lax.rem(y + d, NY),), (lax.rem(y + NY - d, NY),)) for d in range(1, NY)
    ]
    sums = exchanged(1, y, y_others, sums)
    z_others = []
    for d in range(NZ):
        for half in (zh, 1 - zh):
            if d == 0 and half is zh:
                continue
            ahead, behind = lax.rem(z + d, NZ), lax.rem(z + NZ - d, NZ)
            z_others.append((over_z, (None, half, ahead), (half * NZ + behind, half, behind)))
    sums = exchanged(2, zh * NZ + z, z_others, sums)
    scale = jnp.where(
        lanes == 0,
        1.0 / (lengths_ref[0].astype(F32) * WIDTH),
        1.0 / (lengths_ref[1].astype(F32) * WIDTH),
    )
    loss_ref[0, 0] = 0.5 * jnp.sum(sums * scale)

    @pl.when(adds)
    def _():
        for h in range(2):
            sibling_copy(h).wait_send()
        for d in range(NX):
            for flip in range(2):
                if d or flip:
                    loss_row(d, flip).wait_send()

    for copy in sends:
        copy.wait_send()


def on_device(
    latents,
    lengths,
    t_index,
    mod_scale,
    q_weight,
    k_weight,
    v_weight,
    out_weight,
    q_gain,
    k_gain,
    student_weight,
):
    smem = pl.BlockSpec(memory_space=pltpu.SMEM)
    vmem = pl.BlockSpec(memory_space=pltpu.VMEM)
    anywhere = pl.BlockSpec(memory_space=pl.ANY)
    both, loss = pl.pallas_call(
        kernel,
        out_shape=(
            jax.ShapeDtypeStruct((2, 192, ROWS), BF16),
            jax.ShapeDtypeStruct((1, 1), F32),
        ),
        in_specs=[anywhere] * 11,
        out_specs=(vmem, smem),
        scratch_shapes=[
            pltpu.VMEM((CHUNKS, CHUNK, ROWS), BF16),
            pltpu.VMEM((WIDTH, CHUNK), BF16),
            pltpu.VMEM((ROWS, WIDTH), BF16),
            pltpu.VMEM((192, WIDTH), BF16),
            pltpu.VMEM((CHUNKS, ROWS, CHUNK), BF16),
            pltpu.VMEM((CHUNKS, ROWS, CHUNK), BF16),
            pltpu.VMEM((2, NZ, ROWS, HEAD), BF16),
            pltpu.VMEM((2, NY, 2, ROWS, HEAD), BF16),
            pltpu.VMEM((8, 128), F32),
            pltpu.VMEM((2, NZ, ROWS + 16, HEAD), BF16),
            pltpu.VMEM((2, NZ - 1, ROWS + 16, HEAD), BF16),
            pltpu.VMEM((2, 2, CHUNKS, HALF, HEAD), BF16),
            pltpu.VMEM((2, 2, 2, HALF, CHUNK), BF16),
            pltpu.VMEM((CHUNKS, ROWS, CHUNK), BF16),
            pltpu.VMEM((ROWS, CHUNK), BF16),
            pltpu.VMEM((2, CHUNKS, HALF, CHUNK), BF16),
            pltpu.VMEM((CHUNKS, HALF, CHUNK), BF16),
            pltpu.VMEM((CHUNKS, HALF, CHUNK), BF16),
            pltpu.VMEM((NX - 1, 2, HALF, CHUNK), BF16),
            pltpu.VMEM((2, HALF, CHUNK), BF16),
            pltpu.VMEM((HALF, CHUNK), BF16),
            pltpu.VMEM((2, HALF, CHUNK), BF16),
            pltpu.VMEM((ROWS, CHUNK), F32),
            pltpu.VMEM((NZ, ROWS, 2 * HEAD), F32),
            pltpu.VMEM((3, 8, 1, 128), F32),
            pltpu.SMEM((2,), jnp.int32),
            pltpu.SMEM((2,), jnp.int32),
            pltpu.VMEM((1, WIDTH), F32),
            pltpu.VMEM((1, HEAD), F32),
            pltpu.VMEM((1, HEAD), F32),
            pltpu.SemaphoreType.DMA((11,)),
            pltpu.SemaphoreType.DMA((MAX_COPIES,)),
            pltpu.SemaphoreType.DMA((MAX_COPIES,)),
        ],
        compiler_params=pltpu.CompilerParams(
            collective_id=0, has_side_effects=True, vmem_limit_bytes=VMEM_LIMIT
        ),
    )(
        lengths,
        t_index,
        latents.T,
        mod_scale.reshape(1, WIDTH),
        q_weight,
        k_weight,
        v_weight,
        out_weight,
        q_gain.reshape(1, HEAD),
        k_gain.reshape(1, HEAD),
        student_weight,
    )
    return (both[0].T, both[1].T, loss.reshape(()))


def solution(mesh):
    torus = Mesh(
        mesh.devices.reshape(4, 8, 4, 2, 2), ("seq_0", "seq_1", "tp_0", "tp_1", "tp_2")
    )
    in_specs = (
        P(SEQ, TP),
        P(),
        P(),
        P(),
        P(None, TP),
        P(None, TP),
        P(None, TP),
        P(TP, None),
        P(),
        P(),
        P(TP, None),
    )
    out_specs = (P(SEQ, TP), P(SEQ, TP), P())
    return jax.shard_map(
        on_device, mesh=torus, in_specs=in_specs, out_specs=out_specs, check_vma=False
    )
```

```python
import math

import jax
import jax.numpy as jnp
from jax import lax
from jax.experimental import pallas as pl
from jax.experimental.pallas import tpu as pltpu
from jax.sharding import Mesh
from jax.sharding import PartitionSpec as P

SEQ = ("seq_0", "seq_1")
TP = ("tp_0", "tp_1", "tp_2")
MESH = pl.DeviceIdType.MESH
F32, BF16 = jnp.float32, jnp.bfloat16
NX, NY, NZ = 4, 8, 4
ROWS, HALF = 128, 64
CHUNK, CHUNKS = 384, 8
WIDTH, INNER, HEAD = 3072, 1024, 128
EPS = 1e-6
KINETIC = 0.1
STEP = 0.125
EXP_SCALE = math.log2(math.e) / math.sqrt(HEAD)
MAX_COPIES = 250
PARTS = 4
FAR_FIRST = (2, 1, 3)
PART = ROWS // PARTS
VMEM_LIMIT = 67043328


def kernel(
    lengths_hbm,
    t_index_hbm,
    latents_hbm,
    mod_hbm,
    wq_hbm,
    wk_hbm,
    wv_hbm,
    wo_hbm,
    q_gain_hbm,
    k_gain_hbm,
    ws_hbm,
    both_hbm,
    loss_ref,
    xt,
    wqkv,
    wo,
    ws,
    xbuf,
    wcols,
    qbuf,
    kvbuf,
    obuf,
    esend,
    erecv,
    abuf,
    pbuf,
    vbuf,
    v1buf,
    ssend,
    srecv,
    sx_send,
    sx_recv,
    sz_send,
    sz_recv,
    ubuf,
    acc_qkv,
    acc_o,
    lossbuf,
    both_ref,
    lengths_ref,
    t_index_ref,
    mod_ref,
    q_gain_ref,
    k_gain_ref,
    local_sem,
    send_sem,
    recv_sem,
):
    z = lax.axis_index("seq_0")
    y = lax.axis_index("seq_1")
    x = lax.axis_index("tp_0")
    zh = lax.axis_index("tp_1")
    c = lax.axis_index("tp_2")
    other = 1 - c

    loads = [
        pltpu.make_async_copy(latents_hbm, xt.at[2 * x + zh, pl.ds(pl.multiple_of(c * 192, 192), 192), :], local_sem.at[0]),
        pltpu.make_async_copy(wq_hbm, wqkv.at[:, 0:HEAD], local_sem.at[1]),
        pltpu.make_async_copy(wk_hbm, wqkv.at[:, HEAD : 2 * HEAD], local_sem.at[2]),
        pltpu.make_async_copy(wv_hbm, wqkv.at[:, 2 * HEAD : 3 * HEAD], local_sem.at[3]),
        pltpu.make_async_copy(wo_hbm, wo, local_sem.at[4]),
        pltpu.make_async_copy(ws_hbm, ws, local_sem.at[5]),
        pltpu.make_async_copy(lengths_hbm, lengths_ref, local_sem.at[6]),
        pltpu.make_async_copy(t_index_hbm, t_index_ref, local_sem.at[7]),
        pltpu.make_async_copy(mod_hbm, mod_ref, local_sem.at[8]),
        pltpu.make_async_copy(q_gain_hbm, q_gain_ref, local_sem.at[9]),
        pltpu.make_async_copy(k_gain_hbm, k_gain_ref, local_sem.at[10]),
    ]
    for load in loads[:1] + loads[6:]:
        load.start()

    barrier = pltpu.get_barrier_semaphore()
    peers = [{"seq_1": lax.rem(y + d, NY)} for d in range(1, NY)]
    peers += [{"seq_0": lax.rem(z + d, NZ)} for d in range(1, NZ)]
    peers += [{"seq_0": lax.rem(z + d, NZ), "tp_1": 1 - zh} for d in range(NZ)]
    peers += [{"tp_0": lax.rem(x + d, NX)} for d in range(1, NX)]
    peers += [{"tp_0": lax.rem(x + d, NX), "tp_2": other} for d in range(NX)]
    for peer in peers:
        pl.semaphore_signal(barrier, inc=1, device_id=peer, device_id_type=MESH)
    for load in loads[:1] + loads[6:]:
        load.wait()
    pl.semaphore_wait(barrier, len(peers))

    count = [0]
    sends = []

    def slot():
        count[0] += 1
        assert count[0] <= MAX_COPIES
        return count[0] - 1

    def remote(src, dst, k, **where):
        return pltpu.make_async_remote_copy(
            src_ref=src,
            dst_ref=dst,
            send_sem=send_sem.at[k],
            recv_sem=recv_sem.at[k],
            device_id=where,
            device_id_type=MESH,
        )

    def send(src, dst, k, **where):
        copy = remote(src, dst, k, **where)
        copy.start()
        sends.append(copy)

    def arrived(dst, k, **where):
        remote(dst, dst, k, **where).wait_recv()

    def x_at(d):
        return lax.rem(x + d + NX, NX)

    def rows_of(which):
        return pl.ds(pl.multiple_of(which * HALF, HALF), HALF)

    def half_columns(value):
        return jnp.where(c == 0, value[:, 0:192], value[:, 192:384])

    first_length = lengths_ref[0]
    first_t = t_index_ref[0].astype(F32) * STEP
    second_t = t_index_ref[1].astype(F32) * STEP
    row_iota = lax.broadcasted_iota(jnp.int32, (ROWS, 1), 0)
    base = (z * NY + y) * ROWS
    in_first = (base + row_iota) < first_length
    start_times = jnp.where(in_first, first_t, second_t)

    own_chunk = 2 * x + zh

    def piece(chunk, which, h=None):
        start, size = (which * 192, 192) if h is None else (which * 192 + h * 96, 96)
        return xt.at[chunk, pl.ds(pl.multiple_of(start, size), size), :]

    k_z = [slot(), slot()]
    k_x = [[[slot(), slot()] for _ in range(1, NX)] for _ in range(2)]
    k_c = [slot() for _ in range(CHUNKS)]
    for h in range(2):
        send(piece(own_chunk, c, h), piece(own_chunk, c, h), k_z[h], tp_1=1 - zh)
    for d in FAR_FIRST:
        send(piece(own_chunk, c), piece(own_chunk, c), k_x[0][d - 1][0], tp_0=x_at(d))
    send(piece(own_chunk, c), piece(own_chunk, c), k_c[0], tp_2=other)
    for load in loads[1:4]:
        load.start()
    arrivals = [own_chunk]
    far_chunk = 2 * x + 1 - zh
    for h in range(2):
        arrived(piece(far_chunk, c, h), k_z[h], tp_1=1 - zh)
        for d in FAR_FIRST:
            send(piece(far_chunk, c, h), piece(far_chunk, c, h), k_x[1][d - 1][h], tp_0=x_at(d))
    for d in range(1, NX):
        chunk = 2 * x_at(-d) + zh
        arrived(piece(chunk, c), k_x[0][d - 1][0], tp_0=x_at(-d))
        send(piece(chunk, c), piece(chunk, c), k_c[d], tp_2=other)
        arrivals.append(chunk)
    send(piece(far_chunk, c), piece(far_chunk, c), k_c[NX], tp_2=other)
    arrivals.append(far_chunk)
    for load in loads[4:6]:
        load.start()

    for load in loads[1:4]:
        load.wait()

    def project_chunk(number, chunk, state, times, squares):
        modulation = mod_ref[:, pl.ds(pl.multiple_of(chunk * CHUNK, CHUNK), CHUNK)]
        squares = squares + jnp.sum(state * state, axis=1, keepdims=True)
        hidden = (state * (1.0 + times * modulation)).astype(BF16)
        weights = wqkv[pl.ds(pl.multiple_of(chunk * CHUNK, CHUNK), CHUNK), :]
        term = jnp.dot(hidden, weights, preferred_element_type=F32)
        if number == 0:
            acc_qkv[...] = term
        else:
            acc_qkv[...] += term
        return squares, hidden

    squares = jnp.zeros((ROWS, 1), F32)
    own_hidden = None

    def latents_chunk(number, squares):
        chunk = arrivals[number]
        arrived(piece(chunk, other), k_c[number], tp_2=other)
        state = xt[chunk].T
        xbuf[chunk] = state
        return project_chunk(number, chunk, state.astype(F32), start_times, squares)

    for number in range(NX + 1):
        squares, hidden = latents_chunk(number, squares)
        if number == 0:
            own_hidden = hidden
    for d in range(1, NX):
        chunk = 2 * x_at(-d) + 1 - zh
        for h in range(2):
            arrived(piece(chunk, c, h), k_x[1][d - 1][h], tp_0=x_at(-d))
        send(piece(chunk, c), piece(chunk, c), k_c[NX + d], tp_2=other)
        arrivals.append(chunk)
    for number in range(NX + 1, CHUNKS):
        squares, hidden = latents_chunk(number, squares)

    def head_norm(value, gain):
        return (value * lax.rsqrt(jnp.mean(value * value, axis=1, keepdims=True) + EPS) * gain).astype(BF16)

    eye = lax.broadcasted_iota(jnp.int32, (ROWS, ROWS), 0) == lax.broadcasted_iota(
        jnp.int32, (ROWS, ROWS), 1
    )
    lane_iota = lax.broadcasted_iota(jnp.int32, (1, ROWS), 1)

    def attention(e, inverse, while_waiting):
        scaled = acc_qkv[...] * inverse
        qbuf[e, z] = head_norm(scaled[:, 0:HEAD], q_gain_ref[...])
        kvbuf[e, y, 0] = head_norm(scaled[:, HEAD : 2 * HEAD], k_gain_ref[...])
        kvbuf[e, y, 1] = scaled[:, 2 * HEAD : 3 * HEAD].astype(BF16)
        k_ring = [[[slot(), slot()] for _ in range(4)] for _ in range(2)]
        k_q = [slot() for _ in range(1, NZ)]

        def part(owner, which):
            return kvbuf.at[e, owner, which]

        def at(distance):
            return lax.rem(y + distance + NY, NY)

        def pass_on(owner, which, direction, distance, hops):
            target = at(hops if direction == 0 else -hops)
            send(
                part(owner, which), part(owner, which), k_ring[direction][distance - 1][which], seq_1=target
            )

        for hops in (2, 1):
            for which in range(2):
                for direction in range(2):
                    pass_on(y, which, direction, hops, hops)
        for d in range(1, NZ):
            send(qbuf.at[e, z], qbuf.at[e, z], k_q[d - 1], seq_0=lax.rem(z + d, NZ))
        while_waiting[0]()

        came_by = (1, 2, 1, 2)

        def take(distance):
            owners = (at(-distance), at(distance))
            for which in range(2):
                for direction in range(2):
                    if distance == 4 and which != direction:
                        continue
                    hops = came_by[distance - 1]
                    source = at(-hops if direction == 0 else hops)
                    arrived(part(owners[direction], which), k_ring[direction][distance - 1][which], seq_1=source)
                    if distance == 2:
                        if which == direction:
                            pass_on(owners[direction], which, direction, 4, 2)
                        pass_on(owners[direction], which, direction, 3, 1)
            return owners

        queries_from = [lax.rem(z + d, NZ) for d in range(NZ)]

        def block(owner, first):
            keys, values = kvbuf[e, owner, 0], kvbuf[e, owner, 1]
            both = jnp.concatenate([values, jnp.ones_like(values)], axis=1)
            key_first = ((z * NY + owner) * ROWS + lane_iota) < first_length
            for i in range(NZ):
                query_first = ((i * NY + y) * ROWS + row_iota) < first_length
                scores = lax.dot_general(
                    qbuf[e, i], keys, (((1,), (1,)), ((), ())), preferred_element_type=F32
                )
                same = jnp.logical_xor(query_first, jnp.logical_not(key_first))
                weights = jnp.where(same, jnp.exp2(scores * EXP_SCALE), 0.0).astype(BF16)
                term = jnp.dot(weights, both, preferred_element_type=F32)
                if first:
                    acc_o[i] = term
                else:
                    acc_o[i] += term

        near = take(2) + take(1)
        for d in range(1, NZ):
            source = lax.rem(z + NZ - d, NZ)
            arrived(qbuf.at[e, source], k_q[d - 1], seq_0=source)
        block(y, True)
        for owner in near:
            block(owner, False)
        for owner in take(3):
            block(owner, False)
        block(take(4)[0], False)

        k_e = [slot() for _ in range(1, NZ)]
        head16 = lax.broadcasted_iota(jnp.int32, (16, ROWS), 0)

        for i in range(NZ):
            product = acc_o[i]
            total = jnp.sum(jnp.where(eye, product[:, HEAD:], 0.0), axis=0, keepdims=True)
            high = total.astype(BF16).astype(F32)
            low = total - high
            esend[e, i, 0:ROWS, :] = product[:, 0:HEAD].astype(BF16)
            esend[e, i, ROWS : ROWS + 16, :] = jnp.where(
                head16 == 0, high, jnp.where(head16 == 1, low, 0.0)
            ).astype(BF16)
        for d in range(1, NZ):
            target = lax.rem(z + d, NZ)
            send(esend.at[e, target], erecv.at[e, d - 1], k_e[d - 1], seq_0=target)
        while_waiting[1]()

        mixed = esend[e, z].astype(F32)
        for d in range(1, NZ):
            arrived(erecv.at[e, d - 1], k_e[d - 1], seq_0=lax.rem(z + NZ - d, NZ))
            mixed = mixed + erecv[e, d - 1].astype(F32)
        total = mixed[ROWS : ROWS + 1, :] + mixed[ROWS + 1 : ROWS + 2, :]
        column = jnp.sum(jnp.where(eye, total, 0.0), axis=1, keepdims=True)
        return (mixed[0:ROWS, :] / column).astype(BF16)

    def partial_velocity(e, attended, while_waiting, hand_on):
        own = 2 * x + c
        k_a = [[slot(), slot()] for _ in range(NX)]
        abuf[e, own] = attended
        for d in FAR_FIRST:
            send(abuf.at[e, own], abuf.at[e, own], k_a[d][0], tp_0=x_at(d))
        send(abuf.at[e, own], abuf.at[e, own], k_a[0][1], tp_2=other)
        while_waiting()
        for d in range(1, NX):
            part = abuf.at[e, 2 * x_at(-d) + c]
            arrived(part, k_a[d][0], tp_0=x_at(-d))
            send(part, part, k_a[d][1], tp_2=other)
        for d in range(NX):
            arrived(abuf.at[e, 2 * x_at(-d) + other], k_a[d][1], tp_2=other)
        heads = jnp.concatenate([abuf[e, i] for i in range(CHUNKS)], axis=1)
        weights = wcols[...].reshape(INNER, CHUNK)
        for h in range(PARTS):
            rows = heads[h * PART : (h + 1) * PART]
            pbuf[e, 0, h] = jnp.dot(rows, weights, preferred_element_type=F32).astype(BF16)
            hand_on(h)

    def both_partials(e, h):
        return (pbuf[e, 0, h].astype(F32) + pbuf[e, 1, h].astype(F32)).astype(BF16)

    k_w = [[slot(), slot()] for _ in range(NX)]
    k_sc = slot()
    k_sx = [slot() for _ in range(1, NX)]
    k_sz = slot()
    k_su = slot()
    inverse = lax.rsqrt(squares * (1.0 / WIDTH) + EPS)

    def send_columns():
        loads[4].wait()
        for d in range(NX):
            for flip in range(2):
                if d == 0 and flip == 0:
                    continue
                core = c if flip == 0 else other
                columns = pl.ds(pl.multiple_of((2 * x_at(d) + core) * CHUNK, CHUNK), CHUNK)
                send(wo.at[:, columns], wcols.at[2 * x + c], k_w[d][flip], tp_0=x_at(d), tp_2=core)
        wcols[2 * x + c] = wo[:, pl.ds(pl.multiple_of((2 * x + c) * CHUNK, CHUNK), CHUNK)]
        loads[5].wait()
        rows = half_columns(own_hidden.astype(F32)).astype(BF16)
        for j in range(CHUNKS):
            product = jnp.dot(rows, ws[:, j * CHUNK : (j + 1) * CHUNK], preferred_element_type=F32) * inverse
            ssend[0, j] = product[0:HALF].astype(BF16)
            ssend[1, j] = product[HALF:ROWS].astype(BF16)
        send(ssend.at[other], srecv, k_sc, tp_2=other)

    def student_x():
        arrived(srecv, k_sc, tp_2=other)
        for j in range(CHUNKS):
            sx_send[j] = (ssend[c, j].astype(F32) + srecv[j].astype(F32)).astype(BF16)
        for d in range(1, NX):
            send(sx_send.at[pl.ds(2 * x_at(d), 2)], sx_recv.at[d - 1], k_sx[d - 1], tp_0=x_at(d))

    def student_z():
        total = sx_send[pl.ds(2 * x, 2)].astype(F32)
        for d in range(1, NX):
            arrived(sx_recv.at[d - 1], k_sx[d - 1], tp_0=x_at(-d))
            total = total + sx_recv[d - 1].astype(F32)
        sz_send[...] = total.astype(BF16)
        send(sz_send.at[1 - zh], sz_recv, k_sz, tp_1=1 - zh)

    def columns_here():
        for d in range(NX):
            for flip in range(2):
                if d == 0 and flip == 0:
                    continue
                core = c if flip == 0 else other
                arrived(wcols.at[2 * x_at(-d) + core], k_w[d][flip], tp_0=x_at(-d), tp_2=core)

    def student_core():
        arrived(sz_recv, k_sz, tp_1=1 - zh)
        ubuf[c] = (sz_send[zh].astype(F32) + sz_recv[...].astype(F32)).astype(BF16)
        send(ubuf.at[c], ubuf.at[c], k_su, tp_2=other)

    def nothing():
        pass

    attended = attention(0, inverse, (send_columns, student_x))
    k_p = [[slot() for _ in range(PARTS)] for _ in range(2)]

    def to_partner(h):
        send(pbuf.at[0, 0, h], pbuf.at[0, 1, h], k_p[0][h], tp_1=1 - zh)

    partial_velocity(0, attended, columns_here, to_partner)
    student_z()

    own_slot = 2 * x + c
    k_vx = [[slot() for _ in range(1, NX)] for _ in range(PARTS)]
    k_vc = [[slot() for _ in range(NX)] for _ in range(PARTS)]

    def vpart(chunk, h):
        return vbuf.at[chunk, h * PART : (h + 1) * PART, :]

    for h in range(PARTS):
        arrived(pbuf.at[0, 1, h], k_p[0][h], tp_1=1 - zh)
        vbuf[own_slot, h * PART : (h + 1) * PART, :] = both_partials(0, h)
        for d in FAR_FIRST:
            send(vpart(own_slot, h), vpart(own_slot, h), k_vx[h][d - 1], tp_0=x_at(d))
        send(vpart(own_slot, h), vpart(own_slot, h), k_vc[h][0], tp_2=other)
    squares = jnp.zeros((ROWS, 1), F32)
    times = start_times + STEP

    def state_chunk(number, chunk, squares):
        state = (xbuf[chunk].astype(F32) + STEP * vbuf[chunk].astype(F32)).astype(BF16)
        return project_chunk(number, chunk, state.astype(F32), times, squares)[0]

    squares = state_chunk(0, own_slot, squares)
    for h in range(PARTS):
        arrived(vpart(2 * x + other, h), k_vc[h][0], tp_2=other)
    squares = state_chunk(1, 2 * x + other, squares)
    for h in range(PARTS):
        for d in range(1, NX):
            theirs = 2 * x_at(-d) + c
            arrived(vpart(theirs, h), k_vx[h][d - 1], tp_0=x_at(-d))
            send(vpart(theirs, h), vpart(theirs, h), k_vc[h][d], tp_2=other)
    for d in range(1, NX):
        squares = state_chunk(2 * d, 2 * x_at(-d) + c, squares)
    for d in range(1, NX):
        last = 2 * x_at(-d) + other
        for h in range(PARTS):
            arrived(vpart(last, h), k_vc[h][d], tp_2=other)
        squares = state_chunk(2 * d + 1, last, squares)

    inverse = lax.rsqrt(squares * (1.0 / WIDTH) + EPS)
    attended = attention(1, inverse, (student_core, nothing))

    adds, helps = c == zh, c != zh
    k_v1 = [slot() for _ in range(PARTS)]

    def partner_copy(h):
        return remote(pbuf.at[1, 0, h], pbuf.at[1, 1, h], k_p[1][h], tp_1=1 - zh)

    def sibling_copy(h):
        part = v1buf.at[h * PART : (h + 1) * PART, :]
        return remote(part, part, k_v1[h], tp_2=other)

    def to_partner_if_needed(h):
        @pl.when(helps)
        def _():
            partner_copy(h).start()

    partial_velocity(1, attended, nothing, to_partner_if_needed)

    arrived(ubuf.at[other], k_su, tp_2=other)
    student_whole = jnp.concatenate([ubuf[0], ubuf[1]], axis=0).astype(F32)
    start_whole = vbuf[own_chunk].astype(F32)
    lanes = lane_iota
    k_l = [[slot(), slot()] for _ in range(NX)]

    def loss_row(d, flip):
        row = lossbuf.at[0, x]
        return remote(row, row, k_l[d][flip], tp_0=x_at(d), tp_2=c if flip == 0 else other)

    def loss_row_from(d, flip):
        row = lossbuf.at[0, x_at(-d)]
        return remote(row, row, k_l[d][flip], tp_0=x_at(-d), tp_2=c if flip == 0 else other)

    @pl.when(adds)
    def _():
        for h in range(PARTS):
            partner_copy(h).wait_recv()
            v1buf[h * PART : (h + 1) * PART, :] = both_partials(1, h)
            sibling_copy(h).start()
        whole = (0.5 * (start_whole + v1buf[...].astype(F32))).astype(BF16).astype(F32)
        residual = student_whole - whole
        per_token = jnp.sum(
            residual * residual + KINETIC * (student_whole * student_whole), axis=1, keepdims=True
        )
        first_sum = jnp.sum(jnp.where(in_first, per_token, 0.0), axis=0, keepdims=True)
        second_sum = jnp.sum(jnp.where(in_first, 0.0, per_token), axis=0, keepdims=True)
        lossbuf[0, x] = jnp.where(lanes == 0, first_sum, jnp.where(lanes == 1, second_sum, 0.0))
        for d in range(NX):
            for flip in range(2):
                if d or flip:
                    loss_row(d, flip).start()

    both_ref[1] = half_columns(student_whole).T.astype(BF16)

    @pl.when(helps)
    def _():
        for h in range(PARTS):
            sibling_copy(h).wait_recv()
            partner_copy(h).wait_send()
        for d in range(NX):
            loss_row_from(d, 1).wait_recv()

    @pl.when(adds)
    def _():
        for d in range(1, NX):
            loss_row_from(d, 0).wait_recv()

    sums = lossbuf[0, 0]
    for i in range(1, NX):
        sums = sums + lossbuf[0, i]

    out_copy = pltpu.make_async_copy(both_ref, both_hbm, local_sem.at[11])

    def exchanged(stage, own, others, sums):
        lossbuf[stage, own] = sums
        numbers = [slot() for _ in others]
        for number, (where, target, source) in zip(numbers, others):
            send(lossbuf.at[stage, own], lossbuf.at[stage, own], number, **where(target))
        if stage == 1:
            both_ref[0] = half_columns(0.5 * (start_whole + v1buf[...].astype(F32))).T.astype(BF16)
            out_copy.start()
        for number, (where, target, source) in zip(numbers, others):
            index = source[0]
            arrived(lossbuf.at[stage, index], number, **where(source))
        total = lossbuf[stage, 0]
        for i in range(1, 8):
            total = total + lossbuf[stage, i]
        return total

    def over_y(place):
        return {"seq_1": place[0]}

    def over_z(place):
        return {"tp_1": place[1], "seq_0": place[2]}

    y_others = [
        (over_y, (lax.rem(y + d, NY),), (lax.rem(y + NY - d, NY),)) for d in range(1, NY)
    ]
    sums = exchanged(1, y, y_others, sums)
    z_others = []
    for d in range(NZ):
        for half in (zh, 1 - zh):
            if d == 0 and half is zh:
                continue
            ahead, behind = lax.rem(z + d, NZ), lax.rem(z + NZ - d, NZ)
            z_others.append((over_z, (None, half, ahead), (half * NZ + behind, half, behind)))
    sums = exchanged(2, zh * NZ + z, z_others, sums)
    scale = jnp.where(
        lanes == 0,
        1.0 / (lengths_ref[0].astype(F32) * WIDTH),
        1.0 / (lengths_ref[1].astype(F32) * WIDTH),
    )
    loss_ref[0, 0] = 0.5 * jnp.sum(sums * scale)

    @pl.when(adds)
    def _():
        for h in range(PARTS):
            sibling_copy(h).wait_send()
        for d in range(NX):
            for flip in range(2):
                if d or flip:
                    loss_row(d, flip).wait_send()

    out_copy.wait()
    for copy in sends:
        copy.wait_send()


def on_device(
    latents,
    lengths,
    t_index,
    mod_scale,
    q_weight,
    k_weight,
    v_weight,
    out_weight,
    q_gain,
    k_gain,
    student_weight,
):
    smem = pl.BlockSpec(memory_space=pltpu.SMEM)
    anywhere = pl.BlockSpec(memory_space=pl.ANY)
    both, loss = pl.pallas_call(
        kernel,
        out_shape=(
            jax.ShapeDtypeStruct((2, 192, ROWS), BF16),
            jax.ShapeDtypeStruct((1, 1), F32),
        ),
        in_specs=[anywhere] * 11,
        out_specs=(anywhere, smem),
        scratch_shapes=[
            pltpu.VMEM((CHUNKS, CHUNK, ROWS), BF16),
            pltpu.VMEM((WIDTH, CHUNK), BF16),
            pltpu.VMEM((ROWS, WIDTH), BF16),
            pltpu.VMEM((192, WIDTH), BF16),
            pltpu.VMEM((CHUNKS, ROWS, CHUNK), BF16),
            pltpu.VMEM((CHUNKS, ROWS, CHUNK), BF16),
            pltpu.VMEM((2, NZ, ROWS, HEAD), BF16),
            pltpu.VMEM((2, NY, 2, ROWS, HEAD), BF16),
            pltpu.VMEM((8, 128), F32),
            pltpu.VMEM((2, NZ, ROWS + 16, HEAD), BF16),
            pltpu.VMEM((2, NZ - 1, ROWS + 16, HEAD), BF16),
            pltpu.VMEM((2, CHUNKS, ROWS, HEAD), BF16),
            pltpu.VMEM((2, 2, PARTS, PART, CHUNK), BF16),
            pltpu.VMEM((CHUNKS, ROWS, CHUNK), BF16),
            pltpu.VMEM((ROWS, CHUNK), BF16),
            pltpu.VMEM((2, CHUNKS, HALF, CHUNK), BF16),
            pltpu.VMEM((CHUNKS, HALF, CHUNK), BF16),
            pltpu.VMEM((CHUNKS, HALF, CHUNK), BF16),
            pltpu.VMEM((NX - 1, 2, HALF, CHUNK), BF16),
            pltpu.VMEM((2, HALF, CHUNK), BF16),
            pltpu.VMEM((HALF, CHUNK), BF16),
            pltpu.VMEM((2, HALF, CHUNK), BF16),
            pltpu.VMEM((ROWS, CHUNK), F32),
            pltpu.VMEM((NZ, ROWS, 2 * HEAD), F32),
            pltpu.VMEM((3, 8, 1, 128), F32),
            pltpu.VMEM((2, 192, ROWS), BF16),
            pltpu.SMEM((2,), jnp.int32),
            pltpu.SMEM((2,), jnp.int32),
            pltpu.VMEM((1, WIDTH), F32),
            pltpu.VMEM((1, HEAD), F32),
            pltpu.VMEM((1, HEAD), F32),
            pltpu.SemaphoreType.DMA((12,)),
            pltpu.SemaphoreType.DMA((MAX_COPIES,)),
            pltpu.SemaphoreType.DMA((MAX_COPIES,)),
        ],
        compiler_params=pltpu.CompilerParams(
            collective_id=0, has_side_effects=True, vmem_limit_bytes=VMEM_LIMIT
        ),
    )(
        lengths,
        t_index,
        latents.T,
        mod_scale.reshape(1, WIDTH),
        q_weight,
        k_weight,
        v_weight,
        out_weight,
        q_gain.reshape(1, HEAD),
        k_gain.reshape(1, HEAD),
        student_weight,
    )
    return (both[0].T, both[1].T, loss.reshape(()))


def solution(mesh):
    torus = Mesh(
        mesh.devices.reshape(4, 8, 4, 2, 2), ("seq_0", "seq_1", "tp_0", "tp_1", "tp_2")
    )
    in_specs = (
        P(SEQ, TP),
        P(),
        P(),
        P(),
        P(None, TP),
        P(None, TP),
        P(None, TP),
        P(TP, None),
        P(),
        P(),
        P(TP, None),
    )
    out_specs = (P(SEQ, TP), P(SEQ, TP), P())
    return jax.shard_map(
        on_device, mesh=torus, in_specs=in_specs, out_specs=out_specs, check_vma=False
    )
```

```python
import math

import jax
import jax.numpy as jnp
from jax import lax
from jax.experimental import pallas as pl
from jax.experimental.pallas import tpu as pltpu
from jax.sharding import Mesh
from jax.sharding import PartitionSpec as P

SEQ = ("seq_0", "seq_1")
TP = ("tp_0", "tp_1", "tp_2")
MESH = pl.DeviceIdType.MESH
F32, BF16 = jnp.float32, jnp.bfloat16
NX, NY, NZ = 4, 8, 4
ROWS, HALF = 128, 64
CHUNK, CHUNKS = 384, 8
WIDTH, INNER, HEAD = 3072, 1024, 128
EPS = 1e-6
KINETIC = 0.1
STEP = 0.125
EXP_SCALE = math.log2(math.e) / math.sqrt(HEAD)
MAX_COPIES = 250
PARTS = 4
FAR_FIRST = (2, 1, 3)
PART = ROWS // PARTS
VMEM_LIMIT = 67043328


def kernel(
    lengths_hbm,
    t_index_hbm,
    latents_hbm,
    mod_hbm,
    wq_hbm,
    wk_hbm,
    wv_hbm,
    wo_hbm,
    q_gain_hbm,
    k_gain_hbm,
    ws_hbm,
    both_hbm,
    loss_ref,
    xt,
    wqkv,
    wo,
    ws,
    xbuf,
    wcols,
    qbuf,
    kvbuf,
    obuf,
    esend,
    erecv,
    abuf,
    pbuf,
    vbuf,
    v1buf,
    ssend,
    srecv,
    sx_send,
    sx_recv,
    sz_send,
    sz_recv,
    ubuf,
    acc_qkv,
    acc_o,
    lossbuf,
    both_ref,
    lengths_ref,
    t_index_ref,
    mod_ref,
    q_gain_ref,
    k_gain_ref,
    local_sem,
    send_sem,
    recv_sem,
):
    z = lax.axis_index("seq_0")
    y = lax.axis_index("seq_1")
    x = lax.axis_index("tp_0")
    zh = lax.axis_index("tp_1")
    c = lax.axis_index("tp_2")
    other = 1 - c

    loads = [
        pltpu.make_async_copy(latents_hbm, xt.at[2 * x + zh, pl.ds(pl.multiple_of(c * 192, 192), 192), :], local_sem.at[0]),
        pltpu.make_async_copy(wq_hbm, wqkv.at[:, 0:HEAD], local_sem.at[1]),
        pltpu.make_async_copy(wk_hbm, wqkv.at[:, HEAD : 2 * HEAD], local_sem.at[2]),
        pltpu.make_async_copy(wv_hbm, wqkv.at[:, 2 * HEAD : 3 * HEAD], local_sem.at[3]),
        pltpu.make_async_copy(wo_hbm, wo, local_sem.at[4]),
        pltpu.make_async_copy(ws_hbm, ws, local_sem.at[5]),
        pltpu.make_async_copy(lengths_hbm, lengths_ref, local_sem.at[6]),
        pltpu.make_async_copy(t_index_hbm, t_index_ref, local_sem.at[7]),
        pltpu.make_async_copy(mod_hbm, mod_ref, local_sem.at[8]),
        pltpu.make_async_copy(q_gain_hbm, q_gain_ref, local_sem.at[9]),
        pltpu.make_async_copy(k_gain_hbm, k_gain_ref, local_sem.at[10]),
    ]
    for load in loads[:1] + loads[6:]:
        load.start()

    barrier = pltpu.get_barrier_semaphore()
    peers = [{"seq_1": lax.rem(y + d, NY)} for d in range(1, NY)]
    peers += [{"seq_0": lax.rem(z + d, NZ)} for d in range(1, NZ)]
    peers += [{"seq_0": lax.rem(z + d, NZ), "tp_1": 1 - zh} for d in range(NZ)]
    peers += [{"tp_0": lax.rem(x + d, NX)} for d in range(1, NX)]
    peers += [{"tp_0": lax.rem(x + d, NX), "tp_2": other} for d in range(NX)]
    for peer in peers:
        pl.semaphore_signal(barrier, inc=1, device_id=peer, device_id_type=MESH)
    for load in loads[:1] + loads[6:]:
        load.wait()
    pl.semaphore_wait(barrier, len(peers))

    count = [0]
    sends = []

    def slot():
        count[0] += 1
        assert count[0] <= MAX_COPIES
        return count[0] - 1

    def remote(src, dst, k, **where):
        return pltpu.make_async_remote_copy(
            src_ref=src,
            dst_ref=dst,
            send_sem=send_sem.at[k],
            recv_sem=recv_sem.at[k],
            device_id=where,
            device_id_type=MESH,
        )

    def send(src, dst, k, **where):
        copy = remote(src, dst, k, **where)
        copy.start()
        sends.append(copy)

    def arrived(dst, k, **where):
        remote(dst, dst, k, **where).wait_recv()

    def x_at(d):
        return lax.rem(x + d + NX, NX)

    def rows_of(which):
        return pl.ds(pl.multiple_of(which * HALF, HALF), HALF)

    def half_columns(value):
        return jnp.where(c == 0, value[:, 0:192], value[:, 192:384])

    first_length = lengths_ref[0]
    first_t = t_index_ref[0].astype(F32) * STEP
    second_t = t_index_ref[1].astype(F32) * STEP
    row_iota = lax.broadcasted_iota(jnp.int32, (ROWS, 1), 0)
    base = (z * NY + y) * ROWS
    in_first = (base + row_iota) < first_length
    start_times = jnp.where(in_first, first_t, second_t)

    own_chunk = 2 * x + zh

    def piece(chunk, which, h=None):
        start, size = (which * 192, 192) if h is None else (which * 192 + h * 96, 96)
        return xt.at[chunk, pl.ds(pl.multiple_of(start, size), size), :]

    k_z = [slot(), slot()]
    k_x = [[[slot(), slot()] for _ in range(1, NX)] for _ in range(2)]
    k_c = [slot() for _ in range(CHUNKS)]
    for h in range(2):
        send(piece(own_chunk, c, h), piece(own_chunk, c, h), k_z[h], tp_1=1 - zh)
    for d in FAR_FIRST:
        send(piece(own_chunk, c), piece(own_chunk, c), k_x[0][d - 1][0], tp_0=x_at(d))
    send(piece(own_chunk, c), piece(own_chunk, c), k_c[0], tp_2=other)
    for load in loads[1:4]:
        load.start()
    arrivals = [own_chunk]
    far_chunk = 2 * x + 1 - zh
    for h in range(2):
        arrived(piece(far_chunk, c, h), k_z[h], tp_1=1 - zh)
        for d in FAR_FIRST:
            send(piece(far_chunk, c, h), piece(far_chunk, c, h), k_x[1][d - 1][h], tp_0=x_at(d))
    for d in range(1, NX):
        chunk = 2 * x_at(-d) + zh
        arrived(piece(chunk, c), k_x[0][d - 1][0], tp_0=x_at(-d))
        send(piece(chunk, c), piece(chunk, c), k_c[d], tp_2=other)
        arrivals.append(chunk)
    send(piece(far_chunk, c), piece(far_chunk, c), k_c[NX], tp_2=other)
    arrivals.append(far_chunk)
    for load in loads[4:6]:
        load.start()

    for load in loads[1:4]:
        load.wait()

    def project_chunk(number, chunk, state, times, squares):
        modulation = mod_ref[:, pl.ds(pl.multiple_of(chunk * CHUNK, CHUNK), CHUNK)]
        squares = squares + jnp.sum(state * state, axis=1, keepdims=True)
        hidden = (state * (1.0 + times * modulation)).astype(BF16)
        weights = wqkv[pl.ds(pl.multiple_of(chunk * CHUNK, CHUNK), CHUNK), :]
        term = jnp.dot(hidden, weights, preferred_element_type=F32)
        if number == 0:
            acc_qkv[...] = term
        else:
            acc_qkv[...] += term
        return squares, hidden

    squares = jnp.zeros((ROWS, 1), F32)
    own_hidden = None

    def latents_chunk(number, squares):
        chunk = arrivals[number]
        arrived(piece(chunk, other), k_c[number], tp_2=other)
        state = xt[chunk].T
        xbuf[chunk] = state
        return project_chunk(number, chunk, state.astype(F32), start_times, squares)

    for number in range(NX + 1):
        squares, hidden = latents_chunk(number, squares)
        if number == 0:
            own_hidden = hidden
    for d in range(1, NX):
        chunk = 2 * x_at(-d) + 1 - zh
        for h in range(2):
            arrived(piece(chunk, c, h), k_x[1][d - 1][h], tp_0=x_at(-d))
        send(piece(chunk, c), piece(chunk, c), k_c[NX + d], tp_2=other)
        arrivals.append(chunk)
    for number in range(NX + 1, CHUNKS):
        squares, hidden = latents_chunk(number, squares)

    def head_norm(value, gain):
        return (value * lax.rsqrt(jnp.mean(value * value, axis=1, keepdims=True) + EPS) * gain).astype(BF16)

    eye = lax.broadcasted_iota(jnp.int32, (ROWS, ROWS), 0) == lax.broadcasted_iota(
        jnp.int32, (ROWS, ROWS), 1
    )
    lane_iota = lax.broadcasted_iota(jnp.int32, (1, ROWS), 1)

    def attention(e, inverse, while_waiting):
        scaled = acc_qkv[...] * inverse
        qbuf[e, z] = head_norm(scaled[:, 0:HEAD], q_gain_ref[...])
        kvbuf[e, y, 0] = head_norm(scaled[:, HEAD : 2 * HEAD], k_gain_ref[...])
        kvbuf[e, y, 1] = scaled[:, 2 * HEAD : 3 * HEAD].astype(BF16)
        k_ring = [[[slot(), slot()] for _ in range(4)] for _ in range(2)]
        k_q = [slot() for _ in range(1, NZ)]

        def part(owner, which):
            return kvbuf.at[e, owner, which]

        def at(distance):
            return lax.rem(y + distance + NY, NY)

        def pass_on(owner, which, direction, distance, hops):
            target = at(hops if direction == 0 else -hops)
            send(
                part(owner, which), part(owner, which), k_ring[direction][distance - 1][which], seq_1=target
            )

        for hops in (2, 1):
            for which in range(2):
                for direction in range(2):
                    pass_on(y, which, direction, hops, hops)
        for d in range(1, NZ):
            send(qbuf.at[e, z], qbuf.at[e, z], k_q[d - 1], seq_0=lax.rem(z + d, NZ))
        while_waiting[0]()

        came_by = (1, 2, 1, 2)

        def take(distance):
            owners = (at(-distance), at(distance))
            for which in range(2):
                for direction in range(2):
                    if distance == 4 and which != direction:
                        continue
                    hops = came_by[distance - 1]
                    source = at(-hops if direction == 0 else hops)
                    arrived(part(owners[direction], which), k_ring[direction][distance - 1][which], seq_1=source)
                    if distance == 2:
                        if which == direction:
                            pass_on(owners[direction], which, direction, 4, 2)
                        pass_on(owners[direction], which, direction, 3, 1)
            return owners

        queries_from = [lax.rem(z + d, NZ) for d in range(NZ)]

        def block(owner, first):
            keys, values = kvbuf[e, owner, 0], kvbuf[e, owner, 1]
            both = jnp.concatenate([values, jnp.ones_like(values)], axis=1)
            key_first = ((z * NY + owner) * ROWS + lane_iota) < first_length
            for i in range(NZ):
                query_first = ((i * NY + y) * ROWS + row_iota) < first_length
                scores = lax.dot_general(
                    qbuf[e, i], keys, (((1,), (1,)), ((), ())), preferred_element_type=F32
                )
                same = jnp.logical_xor(query_first, jnp.logical_not(key_first))
                weights = jnp.where(same, jnp.exp2(scores * EXP_SCALE), 0.0).astype(BF16)
                term = jnp.dot(weights, both, preferred_element_type=F32)
                if first:
                    acc_o[i] = term
                else:
                    acc_o[i] += term

        near = take(2) + take(1)
        for d in range(1, NZ):
            source = lax.rem(z + NZ - d, NZ)
            arrived(qbuf.at[e, source], k_q[d - 1], seq_0=source)
        block(y, True)
        for owner in near:
            block(owner, False)
        for owner in take(3):
            block(owner, False)
        block(take(4)[0], False)

        k_e = [slot() for _ in range(1, NZ)]
        head16 = lax.broadcasted_iota(jnp.int32, (16, ROWS), 0)

        for i in range(NZ):
            product = acc_o[i]
            total = jnp.sum(jnp.where(eye, product[:, HEAD:], 0.0), axis=0, keepdims=True)
            high = total.astype(BF16).astype(F32)
            low = total - high
            esend[e, i, 0:ROWS, :] = product[:, 0:HEAD].astype(BF16)
            esend[e, i, ROWS : ROWS + 16, :] = jnp.where(
                head16 == 0, high, jnp.where(head16 == 1, low, 0.0)
            ).astype(BF16)
        for d in range(1, NZ):
            target = lax.rem(z + d, NZ)
            send(esend.at[e, target], erecv.at[e, d - 1], k_e[d - 1], seq_0=target)
        while_waiting[1]()

        mixed = esend[e, z].astype(F32)
        for d in range(1, NZ):
            arrived(erecv.at[e, d - 1], k_e[d - 1], seq_0=lax.rem(z + NZ - d, NZ))
            mixed = mixed + erecv[e, d - 1].astype(F32)
        total = mixed[ROWS : ROWS + 1, :] + mixed[ROWS + 1 : ROWS + 2, :]
        column = jnp.sum(jnp.where(eye, total, 0.0), axis=1, keepdims=True)
        return (mixed[0:ROWS, :] / column).astype(BF16)

    def partial_velocity(e, attended, while_waiting, hand_on):
        own = 2 * x + c
        k_a = [[slot(), slot()] for _ in range(NX)]
        abuf[e, own] = attended
        for d in FAR_FIRST:
            send(abuf.at[e, own], abuf.at[e, own], k_a[d][0], tp_0=x_at(d))
        send(abuf.at[e, own], abuf.at[e, own], k_a[0][1], tp_2=other)
        while_waiting()
        for d in range(1, NX):
            part = abuf.at[e, 2 * x_at(-d) + c]
            arrived(part, k_a[d][0], tp_0=x_at(-d))
            send(part, part, k_a[d][1], tp_2=other)
        for d in range(NX):
            arrived(abuf.at[e, 2 * x_at(-d) + other], k_a[d][1], tp_2=other)
        heads = jnp.concatenate([abuf[e, i] for i in range(CHUNKS)], axis=1)
        weights = wcols[...].reshape(INNER, CHUNK)
        partial = jnp.dot(heads, weights, preferred_element_type=F32).astype(BF16)
        for h in range(PARTS):
            pbuf[e, 0, h] = partial[h * PART : (h + 1) * PART]
            hand_on(h)

    def both_partials(e, h):
        return (pbuf[e, 0, h].astype(F32) + pbuf[e, 1, h].astype(F32)).astype(BF16)

    k_w = [[slot(), slot()] for _ in range(NX)]
    k_sc = slot()
    k_sx = [slot() for _ in range(1, NX)]
    k_sz = slot()
    k_su = slot()
    inverse = lax.rsqrt(squares * (1.0 / WIDTH) + EPS)

    def send_columns():
        loads[4].wait()
        for d in range(NX):
            for flip in range(2):
                if d == 0 and flip == 0:
                    continue
                core = c if flip == 0 else other
                columns = pl.ds(pl.multiple_of((2 * x_at(d) + core) * CHUNK, CHUNK), CHUNK)
                send(wo.at[:, columns], wcols.at[2 * x + c], k_w[d][flip], tp_0=x_at(d), tp_2=core)
        wcols[2 * x + c] = wo[:, pl.ds(pl.multiple_of((2 * x + c) * CHUNK, CHUNK), CHUNK)]
        loads[5].wait()
        rows = half_columns(own_hidden.astype(F32)).astype(BF16)
        for j in range(CHUNKS):
            product = jnp.dot(rows, ws[:, j * CHUNK : (j + 1) * CHUNK], preferred_element_type=F32) * inverse
            ssend[0, j] = product[0:HALF].astype(BF16)
            ssend[1, j] = product[HALF:ROWS].astype(BF16)
        send(ssend.at[other], srecv, k_sc, tp_2=other)

    def student_x():
        arrived(srecv, k_sc, tp_2=other)
        for j in range(CHUNKS):
            sx_send[j] = (ssend[c, j].astype(F32) + srecv[j].astype(F32)).astype(BF16)
        for d in range(1, NX):
            send(sx_send.at[pl.ds(2 * x_at(d), 2)], sx_recv.at[d - 1], k_sx[d - 1], tp_0=x_at(d))

    def student_z():
        total = sx_send[pl.ds(2 * x, 2)].astype(F32)
        for d in range(1, NX):
            arrived(sx_recv.at[d - 1], k_sx[d - 1], tp_0=x_at(-d))
            total = total + sx_recv[d - 1].astype(F32)
        sz_send[...] = total.astype(BF16)
        send(sz_send.at[1 - zh], sz_recv, k_sz, tp_1=1 - zh)

    def columns_here():
        for d in range(NX):
            for flip in range(2):
                if d == 0 and flip == 0:
                    continue
                core = c if flip == 0 else other
                arrived(wcols.at[2 * x_at(-d) + core], k_w[d][flip], tp_0=x_at(-d), tp_2=core)

    def student_core():
        arrived(sz_recv, k_sz, tp_1=1 - zh)
        ubuf[c] = (sz_send[zh].astype(F32) + sz_recv[...].astype(F32)).astype(BF16)
        send(ubuf.at[c], ubuf.at[c], k_su, tp_2=other)

    def nothing():
        pass

    attended = attention(0, inverse, (send_columns, student_x))
    k_p = [[slot() for _ in range(PARTS)] for _ in range(2)]

    def to_partner(h):
        send(pbuf.at[0, 0, h], pbuf.at[0, 1, h], k_p[0][h], tp_1=1 - zh)

    partial_velocity(0, attended, columns_here, to_partner)
    student_z()

    own_slot = 2 * x + c
    k_vx = [[slot() for _ in range(1, NX)] for _ in range(PARTS)]
    k_vc = [[slot() for _ in range(NX)] for _ in range(PARTS)]

    def vpart(chunk, h):
        return vbuf.at[chunk, h * PART : (h + 1) * PART, :]

    for h in range(PARTS):
        arrived(pbuf.at[0, 1, h], k_p[0][h], tp_1=1 - zh)
        vbuf[own_slot, h * PART : (h + 1) * PART, :] = both_partials(0, h)
        for d in FAR_FIRST:
            send(vpart(own_slot, h), vpart(own_slot, h), k_vx[h][d - 1], tp_0=x_at(d))
        send(vpart(own_slot, h), vpart(own_slot, h), k_vc[h][0], tp_2=other)
    squares = jnp.zeros((ROWS, 1), F32)
    times = start_times + STEP

    def state_chunk(number, chunk, squares):
        state = (xbuf[chunk].astype(F32) + STEP * vbuf[chunk].astype(F32)).astype(BF16)
        return project_chunk(number, chunk, state.astype(F32), times, squares)[0]

    squares = state_chunk(0, own_slot, squares)
    for h in range(PARTS):
        arrived(vpart(2 * x + other, h), k_vc[h][0], tp_2=other)
    squares = state_chunk(1, 2 * x + other, squares)
    for h in range(PARTS):
        for d in range(1, NX):
            theirs = 2 * x_at(-d) + c
            arrived(vpart(theirs, h), k_vx[h][d - 1], tp_0=x_at(-d))
            send(vpart(theirs, h), vpart(theirs, h), k_vc[h][d], tp_2=other)
    for d in range(1, NX):
        squares = state_chunk(2 * d, 2 * x_at(-d) + c, squares)
    for d in range(1, NX):
        last = 2 * x_at(-d) + other
        for h in range(PARTS):
            arrived(vpart(last, h), k_vc[h][d], tp_2=other)
        squares = state_chunk(2 * d + 1, last, squares)

    inverse = lax.rsqrt(squares * (1.0 / WIDTH) + EPS)
    attended = attention(1, inverse, (student_core, nothing))

    adds, helps = c == zh, c != zh
    k_v1 = [slot() for _ in range(PARTS)]

    def partner_copy(h):
        return remote(pbuf.at[1, 0, h], pbuf.at[1, 1, h], k_p[1][h], tp_1=1 - zh)

    def sibling_copy(h):
        part = v1buf.at[h * PART : (h + 1) * PART, :]
        return remote(part, part, k_v1[h], tp_2=other)

    def to_partner_if_needed(h):
        @pl.when(helps)
        def _():
            partner_copy(h).start()

    partial_velocity(1, attended, nothing, to_partner_if_needed)

    arrived(ubuf.at[other], k_su, tp_2=other)
    student_whole = jnp.concatenate([ubuf[0], ubuf[1]], axis=0).astype(F32)
    start_whole = vbuf[own_chunk].astype(F32)
    lanes = lane_iota
    k_l = [[slot(), slot()] for _ in range(NX)]

    def loss_row(d, flip):
        row = lossbuf.at[0, x]
        return remote(row, row, k_l[d][flip], tp_0=x_at(d), tp_2=c if flip == 0 else other)

    def loss_row_from(d, flip):
        row = lossbuf.at[0, x_at(-d)]
        return remote(row, row, k_l[d][flip], tp_0=x_at(-d), tp_2=c if flip == 0 else other)

    @pl.when(adds)
    def _():
        for h in range(PARTS):
            partner_copy(h).wait_recv()
            v1buf[h * PART : (h + 1) * PART, :] = both_partials(1, h)
            sibling_copy(h).start()
        whole = (0.5 * (start_whole + v1buf[...].astype(F32))).astype(BF16).astype(F32)
        residual = student_whole - whole
        per_token = jnp.sum(
            residual * residual + KINETIC * (student_whole * student_whole), axis=1, keepdims=True
        )
        first_sum = jnp.sum(jnp.where(in_first, per_token, 0.0), axis=0, keepdims=True)
        second_sum = jnp.sum(jnp.where(in_first, 0.0, per_token), axis=0, keepdims=True)
        lossbuf[0, x] = jnp.where(lanes == 0, first_sum, jnp.where(lanes == 1, second_sum, 0.0))
        for d in range(NX):
            for flip in range(2):
                if d or flip:
                    loss_row(d, flip).start()

    both_ref[1] = half_columns(student_whole).T.astype(BF16)

    @pl.when(helps)
    def _():
        for h in range(PARTS):
            sibling_copy(h).wait_recv()
            partner_copy(h).wait_send()
        for d in range(NX):
            loss_row_from(d, 1).wait_recv()

    @pl.when(adds)
    def _():
        for d in range(1, NX):
            loss_row_from(d, 0).wait_recv()

    sums = lossbuf[0, 0]
    for i in range(1, NX):
        sums = sums + lossbuf[0, i]

    out_copy = pltpu.make_async_copy(both_ref, both_hbm, local_sem.at[11])

    def exchanged(stage, own, others, sums):
        lossbuf[stage, own] = sums
        numbers = [slot() for _ in others]
        for number, (where, target, source) in zip(numbers, others):
            send(lossbuf.at[stage, own], lossbuf.at[stage, own], number, **where(target))
        if stage == 1:
            both_ref[0] = half_columns(0.5 * (start_whole + v1buf[...].astype(F32))).T.astype(BF16)
            out_copy.start()
        for number, (where, target, source) in zip(numbers, others):
            index = source[0]
            arrived(lossbuf.at[stage, index], number, **where(source))
        total = lossbuf[stage, 0]
        for i in range(1, 8):
            total = total + lossbuf[stage, i]
        return total

    def over_y(place):
        return {"seq_1": place[0]}

    def over_z(place):
        return {"tp_1": place[1], "seq_0": place[2]}

    y_others = [
        (over_y, (lax.rem(y + d, NY),), (lax.rem(y + NY - d, NY),)) for d in range(1, NY)
    ]
    sums = exchanged(1, y, y_others, sums)
    z_others = []
    for d in range(NZ):
        for half in (zh, 1 - zh):
            if d == 0 and half is zh:
                continue
            ahead, behind = lax.rem(z + d, NZ), lax.rem(z + NZ - d, NZ)
            z_others.append((over_z, (None, half, ahead), (half * NZ + behind, half, behind)))
    sums = exchanged(2, zh * NZ + z, z_others, sums)
    scale = jnp.where(
        lanes == 0,
        1.0 / (lengths_ref[0].astype(F32) * WIDTH),
        1.0 / (lengths_ref[1].astype(F32) * WIDTH),
    )
    loss_ref[0, 0] = 0.5 * jnp.sum(sums * scale)

    @pl.when(adds)
    def _():
        for h in range(PARTS):
            sibling_copy(h).wait_send()
        for d in range(NX):
            for flip in range(2):
                if d or flip:
                    loss_row(d, flip).wait_send()

    out_copy.wait()
    for copy in sends:
        copy.wait_send()


def on_device(
    latents,
    lengths,
    t_index,
    mod_scale,
    q_weight,
    k_weight,
    v_weight,
    out_weight,
    q_gain,
    k_gain,
    student_weight,
):
    smem = pl.BlockSpec(memory_space=pltpu.SMEM)
    anywhere = pl.BlockSpec(memory_space=pl.ANY)
    both, loss = pl.pallas_call(
        kernel,
        out_shape=(
            jax.ShapeDtypeStruct((2, 192, ROWS), BF16),
            jax.ShapeDtypeStruct((1, 1), F32),
        ),
        in_specs=[anywhere] * 11,
        out_specs=(anywhere, smem),
        scratch_shapes=[
            pltpu.VMEM((CHUNKS, CHUNK, ROWS), BF16),
            pltpu.VMEM((WIDTH, CHUNK), BF16),
            pltpu.VMEM((ROWS, WIDTH), BF16),
            pltpu.VMEM((192, WIDTH), BF16),
            pltpu.VMEM((CHUNKS, ROWS, CHUNK), BF16),
            pltpu.VMEM((CHUNKS, ROWS, CHUNK), BF16),
            pltpu.VMEM((2, NZ, ROWS, HEAD), BF16),
            pltpu.VMEM((2, NY, 2, ROWS, HEAD), BF16),
            pltpu.VMEM((8, 128), F32),
            pltpu.VMEM((2, NZ, ROWS + 16, HEAD), BF16),
            pltpu.VMEM((2, NZ - 1, ROWS + 16, HEAD), BF16),
            pltpu.VMEM((2, CHUNKS, ROWS, HEAD), BF16),
            pltpu.VMEM((2, 2, PARTS, PART, CHUNK), BF16),
            pltpu.VMEM((CHUNKS, ROWS, CHUNK), BF16),
            pltpu.VMEM((ROWS, CHUNK), BF16),
            pltpu.VMEM((2, CHUNKS, HALF, CHUNK), BF16),
            pltpu.VMEM((CHUNKS, HALF, CHUNK), BF16),
            pltpu.VMEM((CHUNKS, HALF, CHUNK), BF16),
            pltpu.VMEM((NX - 1, 2, HALF, CHUNK), BF16),
            pltpu.VMEM((2, HALF, CHUNK), BF16),
            pltpu.VMEM((HALF, CHUNK), BF16),
            pltpu.VMEM((2, HALF, CHUNK), BF16),
            pltpu.VMEM((ROWS, CHUNK), F32),
            pltpu.VMEM((NZ, ROWS, 2 * HEAD), F32),
            pltpu.VMEM((3, 8, 1, 128), F32),
            pltpu.VMEM((2, 192, ROWS), BF16),
            pltpu.SMEM((2,), jnp.int32),
            pltpu.SMEM((2,), jnp.int32),
            pltpu.VMEM((1, WIDTH), F32),
            pltpu.VMEM((1, HEAD), F32),
            pltpu.VMEM((1, HEAD), F32),
            pltpu.SemaphoreType.DMA((12,)),
            pltpu.SemaphoreType.DMA((MAX_COPIES,)),
            pltpu.SemaphoreType.DMA((MAX_COPIES,)),
        ],
        compiler_params=pltpu.CompilerParams(
            collective_id=0, has_side_effects=True, vmem_limit_bytes=VMEM_LIMIT
        ),
    )(
        lengths,
        t_index,
        latents.T,
        mod_scale.reshape(1, WIDTH),
        q_weight,
        k_weight,
        v_weight,
        out_weight,
        q_gain.reshape(1, HEAD),
        k_gain.reshape(1, HEAD),
        student_weight,
    )
    return (both[0].T, both[1].T, loss.reshape(()))


def solution(mesh):
    torus = Mesh(
        mesh.devices.reshape(4, 8, 4, 2, 2), ("seq_0", "seq_1", "tp_0", "tp_1", "tp_2")
    )
    in_specs = (
        P(SEQ, TP),
        P(),
        P(),
        P(),
        P(None, TP),
        P(None, TP),
        P(None, TP),
        P(TP, None),
        P(),
        P(),
        P(TP, None),
    )
    out_specs = (P(SEQ, TP), P(SEQ, TP), P())
    return jax.shard_map(
        on_device, mesh=torus, in_specs=in_specs, out_specs=out_specs, check_vma=False
    )
```
